512 devices in a mesh: dp: 4 (over y_lo), seq: 32 (over z, y_hi, core), tensor: 4 (over x).
Axes of the slice: x: 4, y: 8 (y_hi: 2, y_lo: 4; y = y_hi * 4 + y_lo), z: 8, core: 2. Of those that a mesh axis runs over, the one named last changes fastest.
Arguments:
- queries: bfloat16 [4, 16384, 512], P('dp', 'seq', 'tensor'), may hold values from -6 to 6
- values: bfloat16 [4, 16384, 512], P('dp', 'seq', 'tensor'), may hold values from -6 to 6
- filt: float32 [16384, 512], P('seq', 'tensor'), may hold values from -4 to 4
- w_out: bfloat16 [512, 4096], P('tensor'), may hold values from -0.375 to 0.375
- cotangent: bfloat16 [4, 16384, 4096], P('dp', 'seq', 'tensor'), may hold values from -6 to 6
Outputs:
- mixed: bfloat16 [4, 16384, 4096], P('dp', 'seq', 'tensor')
- grad_query: bfloat16 [4, 16384, 512], P('dp', 'seq', 'tensor')
- grad_value: bfloat16 [4, 16384, 512], P('dp', 'seq', 'tensor')
- grad_filt: float32 [16384, 512], P('seq', 'tensor')
The draws below stay inside these ranges and needn't reach their ends.
All inputs are finite; a program needn't handle non-finite values.
Results may differ from the reference program's by a relative error of at most 0.024.
Values may be sent and summed in bfloat16 or wider, within the bound.
No kernel may reach another device: no remote copies, remote signals or barrier semaphores. Data moves between devices by JAX's collectives and lax.ppermute only.
A program may use at most 64 MiB of HBM per device.

```python
import jax
import jax.numpy as jnp

C = 512
DM = 4096
SEQLEN = 16384
BATCH = 4
CH = 128
N_TENSOR = 4


def draw_filt(key, part):
    keys = jax.random.split(jax.random.fold_in(key, 17), 6)
    lags = jnp.arange(SEQLEN, dtype=jnp.float32)[:, None]
    slow_len = jnp.exp(jax.random.uniform(keys[0], (1, C), jnp.float32, jnp.log(0.5 * SEQLEN), jnp.log(4.0 * SEQLEN)))
    fast_len = jnp.exp(jax.random.uniform(keys[1], (1, C), jnp.float32, jnp.log(16.0), jnp.log(48.0)))
    chooser = jax.random.bernoulli(keys[2], 0.5, (1, C))
    decay_len = jnp.where(chooser, slow_len, fast_len)
    envelope = jnp.exp(-lags / decay_len)
    places = jax.random.randint(keys[3], (3, C), 0, SEQLEN).astype(jnp.float32)
    factors = jax.random.uniform(keys[4], (3, C), jnp.float32, 0.5, 0.8)
    for index in range(3):
        envelope = envelope * jnp.where(lags >= places[index][None, :], factors[index][None, :], 1.0)
    noise = jnp.clip(jax.random.normal(keys[5], (SEQLEN, C), jnp.float32), -6.0, 6.0)
    scale = jnp.sqrt(2.0 / jnp.minimum(decay_len, 1.0 * SEQLEN))
    return (scale * envelope * noise).astype(jnp.float32)


def spiked(result, key, source, target, parts, factor):
    def block_of(position):
        return (jnp.arange(result.shape[position]) // (result.shape[position] // parts)).reshape((-1,) + (1,) * (result.ndim - 1 - position))

    near = jax.random.permutation(key, parts)[block_of(target)]
    second = (block_of(target) + parts // 2) % parts
    return jnp.where((block_of(source) == near) | (block_of(source) == second), factor * result, result)


def block_scale(stream_key, shape, pieces, low, high):
    def one(position, shards_of):
        heights = jax.random.uniform(jax.random.fold_in(jax.random.fold_in(stream_key, 6), position), (shards_of,), jnp.float32, low / len(pieces), high / len(pieces))
        return jnp.repeat(jnp.exp(heights), shape[position] // shards_of).reshape((-1,) + (1,) * (len(shape) - position - 1))

    factor_of = one(*pieces[0])
    for cut in pieces[1:]:
        factor_of = factor_of * one(*cut)
    return factor_of


def scatter_about(own_key, dims, scale, reach, cuts=(), kind=jnp.bfloat16):
    gain = block_scale(own_key, dims, cuts, -0.22, 0.18) if cuts else 1.0
    entries = jax.random.normal(own_key, dims, jnp.float32) * scale * gain
    return jnp.minimum(jnp.maximum(entries, -reach), reach).astype(kind)


def heavy_noise(key, extent, deviation, most, cuts, heavy, kind=jnp.bfloat16):
    drawn = deviation * jax.random.normal(key, extent, jnp.float32)
    if cuts:
        drawn = drawn * block_scale(key, extent, cuts, -0.22, 0.18)
    return jnp.clip(spiked(drawn, jax.random.fold_in(key, 3), *heavy), -most, most).astype(kind)


def setup_inputs(seed: int = 0) -> dict:
    key_of = jax.random.split(jax.random.key(seed), 6)
    queries = scatter_about(key_of[0], (BATCH, SEQLEN, C), 1.0, 6.0, ((0, 4), (1, 32), (2, 4)))
    values = scatter_about(key_of[1], (BATCH, SEQLEN, C), 1.0, 6.0, ((0, 4), (1, 32), (2, 4)))
    filt = draw_filt(jax.random.fold_in(key_of[5], 71), 0)
    w_out = heavy_noise(key_of[3], (C, DM), C ** -0.5, 0.375, ((0, 4),), (0, 1, 4, 2.0))
    cotangent = scatter_about(key_of[4], (BATCH, SEQLEN, DM), 1.0, 6.0, ((0, 4), (1, 32), (2, 4)))
    return {"queries": queries, "values": values, "filt": filt, "w_out": w_out, "cotangent": cotangent}


def causal_conv(signal, kernel):
    total = 2 * SEQLEN
    spec = jnp.fft.rfft(signal, n=total, axis=0) * jnp.fft.rfft(kernel, n=total, axis=0)
    return jnp.fft.irfft(spec, n=total, axis=0)[:SEQLEN].astype(jnp.float32)


def causal_corr(grad, kernel):
    total = 2 * SEQLEN
    spec = jnp.fft.rfft(grad, n=total, axis=0) * jnp.conj(jnp.fft.rfft(kernel, n=total, axis=0))
    return jnp.fft.irfft(spec, n=total, axis=0)[:SEQLEN].astype(jnp.float32)


def reference(queries, values, filt, w_out, cotangent):
    kernel = filt.astype(jnp.float32)
    mixed_list = []
    query_list = []
    value_list = []
    grad_filt = jnp.zeros((SEQLEN, C), jnp.float32)
    for batch in range(BATCH):
        query = queries[batch].astype(jnp.float32)
        value = values[batch].astype(jnp.float32)
        conv = causal_conv(value, kernel)
        gated = (query * conv).astype(jnp.bfloat16)
        total = jnp.zeros((SEQLEN, DM), jnp.float32)
        for group in range(N_TENSOR):
            part_sum = jnp.dot(gated[:, group * CH:(group + 1) * CH], w_out[group * CH:(group + 1) * CH],
                               preferred_element_type=jnp.float32).astype(jnp.bfloat16)
            total = total + part_sum.astype(jnp.float32)
        mixed_list.append(total.astype(jnp.bfloat16))
        grad_gated = jnp.dot(cotangent[batch], w_out.T, preferred_element_type=jnp.float32)
        query_list.append((grad_gated * conv).astype(jnp.bfloat16))
        grad_conv = grad_gated * query
        value_list.append(causal_corr(grad_conv, kernel).astype(jnp.bfloat16))
        grad_filt = grad_filt + causal_corr(grad_conv, value)
    return (jnp.stack(mixed_list), jnp.stack(query_list), jnp.stack(value_list), grad_filt)
```

```python
import functools
import math

import jax
import jax.numpy as jnp
import ml_dtypes
import numpy as np
from jax import lax
from jax.experimental import pallas as pl
from jax.experimental.pallas import tpu as pltpu
from jax.sharding import PartitionSpec as P

F32 = jnp.float32
BF16 = jnp.bfloat16
DP = 4
SEQ = 32
ROWS = 4
LANES = 128
SLOTS = 8
HALF = 128


def halves(table):
    high = table.astype(ml_dtypes.bfloat16)
    low = (table - high.astype(np.float64)).astype(ml_dtypes.bfloat16)
    return np.stack([high, low])


@functools.cache
def tables():
    coarse = np.arange(HALF) + 0.5
    row = np.arange(SEQ * SLOTS)
    place = row // SLOTS * ROWS + row % SLOTS % ROWS
    angle = 2 * math.pi / 256 * coarse[:, None] * place[None, :]
    full = np.concatenate([np.cos(angle), -np.sin(angle)])
    first = np.where(row[None, :] % SLOTS < ROWS, full, 0.0)
    second = full - first
    fine = np.arange(LANES)
    angle = 2 * math.pi / LANES * np.outer(fine, fine)
    cos, sin = np.cos(angle), np.sin(angle)
    inner = np.block([[cos, -sin], [sin, cos]])
    angle = 2 * math.pi / 32768 * np.outer(coarse, fine)
    twist = np.stack([np.cos(angle), np.sin(angle)]).astype(np.float32)
    spread = np.zeros((256, 256))
    for channel in range(32):
        for slot in range(SLOTS):
            spread[channel * SLOTS + slot, slot * 32 + channel] = 1.0
    return {
        "fwd_first": halves(first),
        "fwd_second": halves(second),
        "inv_first": halves(first.T / 16384),
        "inv_second": halves(second.T / 16384),
        "inner": halves(inner),
        "inner_t": halves(inner.T),
        "twist": twist,
        "spread": spread.astype(ml_dtypes.bfloat16),
    }


def dot(left, right):
    return jnp.dot(left, right, preferred_element_type=F32)


def split(x):
    high = x.astype(BF16)
    return high, (x - high.astype(F32)).astype(BF16)


def table_dot(table_ref, high, low=None):
    out = dot(table_ref[0], high) + dot(table_ref[1], high)
    if low is not None:
        out = out + dot(table_ref[0], low)
    return out


def dot_table(x, table_ref):
    high, low = split(x)
    return dot(high, table_ref[0]) + dot(low, table_ref[0]) + dot(high, table_ref[1])


def forward(rows, outer_ref, inner_ref, twist_ref):
    coarse = table_dot(outer_ref, rows)
    real, imag = coarse[:HALF], coarse[HALF:]
    cos, sin = twist_ref[0], twist_ref[1]
    turned = jnp.concatenate([real * cos + imag * sin, imag * cos - real * sin], axis=1)
    return dot_table(turned, inner_ref)


def inverse_inner(real, imag, inner_t_ref, twist_ref):
    coarse = dot_table(jnp.concatenate([real, imag], axis=1), inner_t_ref)
    real, imag = coarse[:, :LANES], coarse[:, LANES:]
    cos, sin = twist_ref[0], twist_ref[1]
    return split(jnp.concatenate([real * cos - imag * sin, imag * cos + real * sin], axis=0))


def pack_inputs(values_ref, filt_ref, spread_ref, out_ref):
    dp = lax.axis_index("dp")
    start = pl.multiple_of(dp * LANES, LANES)
    quarter = filt_ref[pl.ds(start, LANES), :].T
    tiles = [values_ref[q * LANES:(q + 1) * LANES, :].astype(F32).T.astype(BF16) for q in range(ROWS)]
    tiles += [jnp.where(dp == q, quarter, 0.0).astype(BF16) for q in range(DP)]
    for part in range(4):
        block = jnp.concatenate([tile[part * 32:(part + 1) * 32] for tile in tiles], axis=0)
        out_ref[part * 256:(part + 1) * 256, :] = dot(spread_ref[...], block).astype(BF16)


def convolve(got_ref, first_ref, second_ref, inv_ref, inner_ref, inner_t_ref, twist_ref, conv_ref, vspec_ref, fspec_ref):
    size = SEQ * SLOTS
    parts = [got_ref[b * size:(b + 1) * size, :] for b in range(DP)]
    filt = ((parts[0].astype(F32) + parts[1].astype(F32)) + (parts[2].astype(F32) + parts[3].astype(F32))).astype(BF16)
    fspec = forward(filt, second_ref, inner_ref, twist_ref)
    fspec_ref[...] = fspec
    f_real, f_imag = fspec[:, :LANES], fspec[:, LANES:]
    for b in range(DP):
        vspec = forward(parts[b], first_ref, inner_ref, twist_ref)
        vspec_ref[b] = vspec
        v_real, v_imag = vspec[:, :LANES], vspec[:, LANES:]
        high, low = inverse_inner(
            v_real * f_real - v_imag * f_imag, v_real * f_imag + v_imag * f_real, inner_t_ref, twist_ref
        )
        conv_ref[b * size:(b + 1) * size, :] = table_dot(inv_ref, high, low).astype(BF16)


def partial_grads(cot_ref, *refs):
    count = len(refs) // 2
    cot = cot_ref[...]
    for w_ref, out_ref in zip(refs[:count], refs[count:]):
        out_ref[...] = lax.dot_general(
            cot, w_ref[...], (((1,), (1,)), ((), ())), preferred_element_type=F32
        ).astype(BF16)


def pack_grads(*refs):
    query_ref, conv_ref, spread_ref = refs[:3]
    pieces, (out_ref, grad_ref) = refs[3:-2], refs[-2:]
    grad = pieces[0][...].astype(F32)
    for piece in pieces[1:]:
        grad = grad + piece[...].astype(F32)
    grad_ref[...] = grad
    grad_conv = grad * query_ref[...].astype(F32)
    tiles = [grad_conv[q * LANES:(q + 1) * LANES, :].T.astype(BF16) for q in range(ROWS)]
    spread = spread_ref[:, 128:]
    for part in range(4):
        block = jnp.concatenate([tile[part * 32:(part + 1) * 32] for tile in tiles], axis=0)
        out_ref[part * 256:(part + 1) * 256, :] = (
            dot(spread, block) + conv_ref[part * 256:(part + 1) * 256, :].astype(F32)
        ).astype(BF16)


def gather_half(got_ref, gather):
    blocks = [dot(gather, got_ref[part * 256:(part + 1) * 256, :]) for part in range(4)]
    return [
        jnp.concatenate([block[q * 32:(q + 1) * 32] for block in blocks], axis=0).T for q in range(gather.shape[0] // 32)
    ]


def unpack_conv(got_ref, query_ref, grad_ref, gather_ref, gated_ref, grad_query_ref):
    for q, conv in enumerate(gather_half(got_ref, gather_ref[:128, :])):
        rows = slice(q * LANES, (q + 1) * LANES)
        gated_ref[rows, :] = (query_ref[rows, :].astype(F32) * conv).astype(BF16)
        grad_query_ref[rows, :] = (grad_ref[rows, :] * conv).astype(BF16)


def correlate(
    got_ref, vspec_ref, fspec_ref, second_ref, inv_first_ref, inv_second_ref, inner_ref, inner_t_ref, twist_ref, out_ref
):
    size = SEQ * SLOTS
    f_real, f_imag = fspec_ref[:, :LANES], fspec_ref[:, LANES:]
    sum_real = sum_imag = None
    inner = []
    for b in range(DP):
        spec = forward(got_ref[b * size:(b + 1) * size, :], second_ref, inner_ref, twist_ref)
        real, imag = spec[:, :LANES], spec[:, LANES:]
        v_real, v_imag = vspec_ref[b, :, :LANES], vspec_ref[b, :, LANES:]
        part_real = real * v_real + imag * v_imag
        part_imag = imag * v_real - real * v_imag
        sum_real = part_real if b == 0 else sum_real + part_real
        sum_imag = part_imag if b == 0 else sum_imag + part_imag
        inner.append(
            inverse_inner(
                real * f_real + imag * f_imag, imag * f_real - real * f_imag, inner_t_ref, twist_ref
            )
        )
    filt = table_dot(inv_second_ref, *inverse_inner(sum_real, sum_imag, inner_t_ref, twist_ref))
    for b in range(DP):
        out_ref[b * size:(b + 1) * size, :] = (table_dot(inv_first_ref, *inner[b]) + filt).astype(BF16)


def unpack_grads(got_ref, gather_ref, value_ref, filt_ref):
    tiles = gather_half(got_ref, gather_ref[...])
    for q in range(ROWS):
        value_ref[q * LANES:(q + 1) * LANES, :] = tiles[q].astype(BF16)
        filt_ref[q * LANES:(q + 1) * LANES, :] = tiles[ROWS + q]


def project(*refs):
    out_ref = refs[-1]
    count = (len(refs) - 1) // 2
    total = dot(refs[0][...], refs[count][...])
    for k in range(1, count):
        total = total + dot(refs[k][...], refs[count + k][...])
    out_ref[...] = total.astype(BF16)


def call(kernel, outs, *operands):
    single = not isinstance(outs, list)
    return pl.pallas_call(
        kernel,
        out_shape=outs if not single else outs,
        name=kernel.__name__,
        compiler_params=pltpu.CompilerParams(vmem_limit_bytes=40 * 1024 * 1024),
    )(*operands)


def exchange(message):
    shape = message.shape
    message = message.reshape(DP * SEQ, SLOTS, LANES)
    return lax.all_to_all(message, ("dp", "seq"), split_axis=0, concat_axis=0, tiled=True).reshape(shape)


def shifted(array, distance, count):
    return lax.ppermute(array, "tensor", [(i, (i + distance) % count) for i in range(count)])


def per_device(queries, values, filt, w_out, cotangent, count):
    t = tables()
    query = queries[0]
    length, width = query.shape
    features = cotangent.shape[2]
    rank = lax.axis_index("tensor")
    message = jax.ShapeDtypeStruct((DP * SEQ * SLOTS, LANES), BF16)
    signal = jax.ShapeDtypeStruct((length, width), BF16)

    columns = []
    for d in range(count):
        piece = lax.dynamic_slice(w_out, (0, (rank + d) % count * features), (width, features))
        columns.append(shifted(piece, d, count) if d else piece)

    got = exchange(call(pack_inputs, message, values[0], filt, t["spread"]))
    conv, value_spec, filt_spec = call(
        convolve,
        [
            message,
            jax.ShapeDtypeStruct((DP, HALF, 2 * LANES), F32),
            jax.ShapeDtypeStruct((HALF, 2 * LANES), F32),
        ],
        got, t["fwd_first"], t["fwd_second"], t["inv_first"], t["inner"], t["inner_t"], t["twist"],
    )
    partial = call(partial_grads, [signal] * count, cotangent[0], *columns)
    partial = [shifted(p, -d, count) if d else p for d, p in enumerate(partial)]
    outgoing, grad_gated = call(
        pack_grads, [message, jax.ShapeDtypeStruct((length, width), F32)], query, conv, t["spread"], *partial
    )
    got = exchange(outgoing)
    gated, grad_query = call(unpack_conv, [signal, signal], got, query, grad_gated, t["spread"].T)
    gathered = [shifted(gated, d, count) if d else gated for d in range(count)]
    got = exchange(
        call(
            correlate, message, got, value_spec, filt_spec, t["fwd_second"], t["inv_first"], t["inv_second"],
            t["inner"], t["inner_t"], t["twist"],
        )
    )
    grad_value, grad_filt = call(
        unpack_grads, [signal, jax.ShapeDtypeStruct((length, width), F32)], got, t["spread"].T
    )
    mixed = call(project, jax.ShapeDtypeStruct((length, features), BF16), *gathered, *columns)
    return (mixed[None], grad_query[None], grad_value[None], grad_filt)


def solution(mesh):
    placed = (
        P("dp", "seq", "tensor"),
        P("dp", "seq", "tensor"),
        P("seq", "tensor"),
        P("tensor", None),
        P("dp", "seq", "tensor"),
    )
    return jax.shard_map(
        functools.partial(per_device, count=mesh.shape["tensor"]),
        mesh=mesh,
        in_specs=placed,
        out_specs=(
            P("dp", "seq", "tensor"),
            P("dp", "seq", "tensor"),
            P("dp", "seq", "tensor"),
            P("seq", "tensor"),
        ),
        check_vma=False,
    )
```

```python
import functools
import math

import jax
import jax.numpy as jnp
import ml_dtypes
import numpy as np
from jax import lax
from jax.experimental import pallas as pl
from jax.experimental.pallas import tpu as pltpu
from jax.sharding import PartitionSpec as P

F32 = jnp.float32
BF16 = jnp.bfloat16
DP = 4
SEQ = 32
ROWS = 4
LANES = 128
SLOTS = 8
HALF = 128


def halves(table):
    high = table.astype(ml_dtypes.bfloat16)
    low = (table - high.astype(np.float64)).astype(ml_dtypes.bfloat16)
    return np.stack([high, low])


@functools.cache
def tables():
    coarse = np.arange(HALF) + 0.5
    row = np.arange(SEQ * SLOTS)
    place = row // SLOTS * ROWS + row % SLOTS % ROWS
    angle = 2 * math.pi / 256 * coarse[:, None] * place[None, :]
    full = np.concatenate([np.cos(angle), -np.sin(angle)])
    first = np.where(row[None, :] % SLOTS < ROWS, full, 0.0)
    second = full - first
    fine = np.arange(LANES)
    angle = 2 * math.pi / LANES * np.outer(fine, fine)
    cos, sin = np.cos(angle), np.sin(angle)
    inner = np.block([[cos, -sin], [sin, cos]])
    angle = 2 * math.pi / 32768 * np.outer(coarse, fine)
    twist = np.stack([np.cos(angle), np.sin(angle)]).astype(np.float32)
    spread = np.zeros((256, 256))
    for channel in range(32):
        for slot in range(SLOTS):
            spread[channel * SLOTS + slot, slot * 32 + channel] = 1.0
    return {
        "fwd_first": halves(first),
        "fwd_second": halves(second),
        "inv_first": halves(first.T / 16384),
        "inv_second": halves(second.T / 16384),
        "inner": halves(inner),
        "inner_t": halves(inner.T),
        "twist": twist,
        "spread": spread.astype(ml_dtypes.bfloat16),
    }


def dot(left, right):
    return jnp.dot(left, right, preferred_element_type=F32)


def split(x):
    high = x.astype(BF16)
    return high, (x - high.astype(F32)).astype(BF16)


def table_dot(table_ref, high, low=None):
    out = dot(table_ref[0], high) + dot(table_ref[1], high)
    if low is not None:
        out = out + dot(table_ref[0], low)
    return out


def dot_table(x, table_ref):
    high, low = split(x)
    return dot(high, table_ref[0]) + dot(low, table_ref[0]) + dot(high, table_ref[1])


def forward(rows, outer_ref, inner_ref, twist_ref):
    coarse = table_dot(outer_ref, rows)
    real, imag = coarse[:HALF], coarse[HALF:]
    cos, sin = twist_ref[0], twist_ref[1]
    turned = jnp.concatenate([real * cos + imag * sin, imag * cos - real * sin], axis=1)
    return dot_table(turned, inner_ref)


def inverse_inner(real, imag, inner_t_ref, twist_ref):
    coarse = dot_table(jnp.concatenate([real, imag], axis=1), inner_t_ref)
    real, imag = coarse[:, :LANES], coarse[:, LANES:]
    cos, sin = twist_ref[0], twist_ref[1]
    return split(jnp.concatenate([real * cos - imag * sin, imag * cos + real * sin], axis=0))


def pack_inputs(values_ref, filt_ref, spread_ref, out_ref):
    dp = lax.axis_index("dp")
    start = pl.multiple_of(dp * LANES, LANES)
    quarter = filt_ref[pl.ds(start, LANES), :].T
    tiles = [values_ref[q * LANES:(q + 1) * LANES, :].astype(F32).T.astype(BF16) for q in range(ROWS)]
    tiles += [jnp.where(dp == q, quarter, 0.0).astype(BF16) for q in range(DP)]
    for part in range(4):
        block = jnp.concatenate([tile[part * 32:(part + 1) * 32] for tile in tiles], axis=0)
        out_ref[part * 256:(part + 1) * 256, :] = dot(spread_ref[...], block).astype(BF16)


def convolve(got_ref, first_ref, second_ref, inv_ref, inner_ref, inner_t_ref, twist_ref, conv_ref, vspec_ref, fspec_ref):
    size = SEQ * SLOTS
    parts = [got_ref[b * size:(b + 1) * size, :] for b in range(DP)]
    filt = ((parts[0].astype(F32) + parts[1].astype(F32)) + (parts[2].astype(F32) + parts[3].astype(F32))).astype(BF16)
    fspec = forward(filt, second_ref, inner_ref, twist_ref)
    fspec_ref[...] = fspec
    f_real, f_imag = fspec[:, :LANES], fspec[:, LANES:]
    for b in range(DP):
        vspec = forward(parts[b], first_ref, inner_ref, twist_ref)
        vspec_ref[b] = vspec
        v_real, v_imag = vspec[:, :LANES], vspec[:, LANES:]
        high, low = inverse_inner(
            v_real * f_real - v_imag * f_imag, v_real * f_imag + v_imag * f_real, inner_t_ref, twist_ref
        )
        conv_ref[b * size:(b + 1) * size, :] = table_dot(inv_ref, high, low).astype(BF16)


def partial_grads(cot_ref, *refs):
    count = len(refs) // 2
    cot = cot_ref[...]
    for w_ref, out_ref in zip(refs[:count], refs[count:]):
        out_ref[...] = lax.dot_general(
            cot, w_ref[...], (((1,), (1,)), ((), ())), preferred_element_type=F32
        ).astype(BF16)


def pack_grads(*refs):
    query_ref, conv_ref, spread_ref = refs[:3]
    pieces, (out_ref, grad_ref) = refs[3:-2], refs[-2:]
    grad = pieces[0][...].astype(F32)
    for piece in pieces[1:]:
        grad = grad + piece[...].astype(F32)
    grad_ref[...] = grad
    grad_conv = grad * query_ref[...].astype(F32)
    tiles = [grad_conv[q * LANES:(q + 1) * LANES, :].T.astype(BF16) for q in range(ROWS)]
    spread = spread_ref[:, 128:]
    for part in range(4):
        block = jnp.concatenate([tile[part * 32:(part + 1) * 32] for tile in tiles], axis=0)
        out_ref[part * 256:(part + 1) * 256, :] = (
            dot(spread, block) + conv_ref[part * 256:(part + 1) * 256, :].astype(F32)
        ).astype(BF16)


def gather_half(got_ref, gather):
    blocks = [dot(gather, got_ref[part * 256:(part + 1) * 256, :]) for part in range(4)]
    return [
        jnp.concatenate([block[q * 32:(q + 1) * 32] for block in blocks], axis=0).T for q in range(gather.shape[0] // 32)
    ]


def unpack_conv(got_ref, query_ref, grad_ref, gather_ref, gated_ref, grad_query_ref):
    for q, conv in enumerate(gather_half(got_ref, gather_ref[:128, :])):
        rows = slice(q * LANES, (q + 1) * LANES)
        gated_ref[rows, :] = (query_ref[rows, :].astype(F32) * conv).astype(BF16)
        grad_query_ref[rows, :] = (grad_ref[rows, :] * conv).astype(BF16)


def correlate(
    got_ref, vspec_ref, fspec_ref, second_ref, inv_first_ref, inv_second_ref, inner_ref, inner_t_ref, twist_ref, out_ref
):
    size = SEQ * SLOTS
    f_real, f_imag = fspec_ref[:, :LANES], fspec_ref[:, LANES:]
    sum_real = sum_imag = None
    inner = []
    for b in range(DP):
        spec = forward(got_ref[b * size:(b + 1) * size, :], second_ref, inner_ref, twist_ref)
        real, imag = spec[:, :LANES], spec[:, LANES:]
        v_real, v_imag = vspec_ref[b, :, :LANES], vspec_ref[b, :, LANES:]
        part_real = real * v_real + imag * v_imag
        part_imag = imag * v_real - real * v_imag
        sum_real = part_real if b == 0 else sum_real + part_real
        sum_imag = part_imag if b == 0 else sum_imag + part_imag
        inner.append(
            inverse_inner(
                real * f_real + imag * f_imag, imag * f_real - real * f_imag, inner_t_ref, twist_ref
            )
        )
    filt = table_dot(inv_second_ref, *inverse_inner(sum_real, sum_imag, inner_t_ref, twist_ref))
    for b in range(DP):
        out_ref[b * size:(b + 1) * size, :] = (table_dot(inv_first_ref, *inner[b]) + filt).astype(BF16)


def unpack_grads(got_ref, gather_ref, value_ref, filt_ref):
    tiles = gather_half(got_ref, gather_ref[...])
    for q in range(ROWS):
        value_ref[q * LANES:(q + 1) * LANES, :] = tiles[q].astype(BF16)
        filt_ref[q * LANES:(q + 1) * LANES, :] = tiles[ROWS + q]


def project(*refs):
    out_ref = refs[-1]
    count = (len(refs) - 1) // 2
    total = dot(refs[0][...], refs[count][...])
    for k in range(1, count):
        total = total + dot(refs[k][...], refs[count + k][...])
    out_ref[...] = total.astype(BF16)


COVER = pl.CostEstimate(flops=40_000_000_000, transcendentals=0, bytes_accessed=40_000_000)
COVERS = {"pack_inputs": COVER, "partial_grads": COVER}


def call(kernel, outs, *operands):
    return pl.pallas_call(
        kernel,
        out_shape=outs,
        name=kernel.__name__,
        cost_estimate=COVERS.get(kernel.__name__),
        compiler_params=pltpu.CompilerParams(vmem_limit_bytes=40 * 1024 * 1024),
    )(*operands)


def exchange(message):
    shape = message.shape
    message = message.reshape(DP * SEQ, SLOTS, LANES)
    return lax.all_to_all(message, ("dp", "seq"), split_axis=0, concat_axis=0, tiled=True).reshape(shape)


def shifted(array, distance, count):
    return lax.ppermute(array, "tensor", [(i, (i + distance) % count) for i in range(count)])


def per_device(queries, values, filt, w_out, cotangent, count):
    t = tables()
    query = queries[0]
    length, width = query.shape
    features = cotangent.shape[2]
    rank = lax.axis_index("tensor")
    message = jax.ShapeDtypeStruct((DP * SEQ * SLOTS, LANES), BF16)
    signal = jax.ShapeDtypeStruct((length, width), BF16)

    columns = []
    for d in range(count):
        piece = lax.dynamic_slice(w_out, (0, (rank + d) % count * features), (width, features))
        columns.append(shifted(piece, d, count) if d else piece)

    got = exchange(call(pack_inputs, message, values[0], filt, t["spread"]))
    conv, value_spec, filt_spec = call(
        convolve,
        [
            message,
            jax.ShapeDtypeStruct((DP, HALF, 2 * LANES), F32),
            jax.ShapeDtypeStruct((HALF, 2 * LANES), F32),
        ],
        got, t["fwd_first"], t["fwd_second"], t["inv_first"], t["inner"], t["inner_t"], t["twist"],
    )
    partial = call(partial_grads, [signal] * count, cotangent[0], *columns)
    partial = [shifted(p, -d, count) if d else p for d, p in enumerate(partial)]
    outgoing, grad_gated = call(
        pack_grads, [message, jax.ShapeDtypeStruct((length, width), F32)], query, conv, t["spread"], *partial
    )
    got = exchange(outgoing)
    gated, grad_query = call(unpack_conv, [signal, signal], got, query, grad_gated, t["spread"].T)
    gathered = [shifted(gated, d, count) if d else gated for d in range(count)]
    got = exchange(
        call(
            correlate, message, got, value_spec, filt_spec, t["fwd_second"], t["inv_first"], t["inv_second"],
            t["inner"], t["inner_t"], t["twist"],
        )
    )
    grad_value, grad_filt = call(
        unpack_grads, [signal, jax.ShapeDtypeStruct((length, width), F32)], got, t["spread"].T
    )
    mixed = call(project, jax.ShapeDtypeStruct((length, features), BF16), *gathered, *columns)
    return (mixed[None], grad_query[None], grad_value[None], grad_filt)


def solution(mesh):
    placed = (
        P("dp", "seq", "tensor"),
        P("dp", "seq", "tensor"),
        P("seq", "tensor"),
        P("tensor", None),
        P("dp", "seq", "tensor"),
    )
    return jax.shard_map(
        functools.partial(per_device, count=mesh.shape["tensor"]),
        mesh=mesh,
        in_specs=placed,
        out_specs=(
            P("dp", "seq", "tensor"),
            P("dp", "seq", "tensor"),
            P("dp", "seq", "tensor"),
            P("seq", "tensor"),
        ),
        check_vma=False,
    )
```

```python
import functools
import math

import jax
import jax.numpy as jnp
import ml_dtypes
import numpy as np
from jax import lax
from jax.experimental import pallas as pl
from jax.experimental.pallas import tpu as pltpu
from jax.sharding import PartitionSpec as P

F32 = jnp.float32
BF16 = jnp.bfloat16
DP = 4
SEQ = 32
ROWS = 4
LANES = 128
CHUNK = 256
HALVES = 256
SLOTS = 8
TURN = 18
HALF = 128


def narrow(table):
    return table.astype(ml_dtypes.bfloat16)


@functools.cache
def tables():
    coarse = np.arange(HALF) + 0.5
    row = np.arange(SEQ * SLOTS)

    def outer(turn):
        place = (row // SLOTS + turn) % SEQ * ROWS + row % SLOTS % ROWS
        angle = 2 * math.pi / 256 * coarse[:, None] * place[None, :]
        full = np.concatenate([np.cos(angle), -np.sin(angle)])
        first = np.where(row[None, :] % SLOTS < ROWS, full, 0.0)
        return first, full - first

    first, second = outer(0)
    turned_first, turned_second = outer(TURN)
    fine = np.arange(LANES)
    angle = 2 * math.pi / LANES * np.outer(fine, fine)
    cos, sin = np.cos(angle), np.sin(angle)
    inner = np.block([[cos, -sin], [sin, cos]])
    angle = 2 * math.pi / 32768 * np.outer(coarse, fine)
    twist = np.stack([np.cos(angle), np.sin(angle)]).astype(np.float32)
    spread, turned_spread = np.zeros((256, 256)), np.zeros((256, 256))
    for channel in range(32):
        for slot in range(SLOTS):
            spread[channel * SLOTS + slot, slot * 32 + channel] = 1.0
            turned_spread[channel * SLOTS + slot, slot * 32 + (channel + TURN) % 32] = 1.0
    return {
        "turned_first": narrow(turned_first),
        "turned_second": narrow(turned_second),
        "fwd_second": narrow(second),
        "inv_first": narrow(first.T / 16384),
        "inv_second": narrow(second.T / 16384),
        "inner": narrow(inner),
        "inner_t": narrow(inner.T),
        "twist": twist,
        "spread": narrow(spread),
        "turned_spread": narrow(turned_spread),
    }


def dot(left, right):
    return jnp.dot(left, right, preferred_element_type=F32)


def split(x):
    high = x.astype(BF16)
    return high, (x - high.astype(F32)).astype(BF16)


def table_dot(table_ref, high, low=None):
    out = dot(table_ref[...], high)
    if low is not None:
        out = out + dot(table_ref[...], low)
    return out


def dot_table(x, table_ref):
    high, low = split(x)
    return dot(high, table_ref[...]) + dot(low, table_ref[...])


def lanes(tiles):
    return jnp.concatenate(tiles, axis=1)


def rows(tiles):
    return jnp.concatenate(tiles, axis=0)


def forward(signals, outer_ref, inner_ref, twist_ref):
    count = signals.shape[1] // LANES
    coarse = table_dot(outer_ref, signals)
    cos, sin = lanes([twist_ref[0]] * count), lanes([twist_ref[1]] * count)
    real, imag = coarse[:HALF], coarse[HALF:]
    real, imag = real * cos + imag * sin, imag * cos - real * sin
    cuts = [slice(k * LANES, (k + 1) * LANES) for k in range(count)]
    return dot_table(rows([lanes([real[:, cut], imag[:, cut]]) for cut in cuts]), inner_ref)


def inverse_inner(spectra, inner_t_ref, twist_ref):
    count = spectra.shape[0] // HALF
    coarse = dot_table(spectra, inner_t_ref)
    cos, sin = twist_ref[0], twist_ref[1]
    out = []
    for k in range(count):
        real, imag = coarse[k * HALF:(k + 1) * HALF, :LANES], coarse[k * HALF:(k + 1) * HALF, LANES:]
        out.append(rows([real * cos - imag * sin, imag * cos + real * sin]))
    return split(lanes(out))


def pack_inputs(values_ref, filt_ref, spread_ref, out_ref):
    dp = lax.axis_index("dp")
    start = pl.multiple_of(dp * LANES, LANES)
    quarter = filt_ref[pl.ds(start, LANES), :].T
    tiles = [values_ref[q * LANES:(q + 1) * LANES, :].astype(F32).T.astype(BF16) for q in range(ROWS)]
    tiles += [jnp.where(dp == q, quarter, 0.0).astype(BF16) for q in range(DP)]
    for part in range(4):
        block = jnp.concatenate([tile[part * 32:(part + 1) * 32] for tile in tiles], axis=0)
        out_ref[part * 256:(part + 1) * 256, :] = dot(spread_ref[...], block).astype(BF16)


def convolve(got_ref, first_ref, second_ref, inv_ref, inner_ref, inner_t_ref, twist_ref, conv_ref, vspec_ref, fspec_ref):
    size = SEQ * SLOTS
    parts = [got_ref[b * size:(b + 1) * size, :] for b in range(DP)]
    filt = ((parts[0].astype(F32) + parts[1].astype(F32)) + (parts[2].astype(F32) + parts[3].astype(F32))).astype(BF16)
    fspec = forward(filt, second_ref, inner_ref, twist_ref)
    fspec_ref[...] = fspec
    f_real, f_imag = fspec[:, :LANES], fspec[:, LANES:]
    vspec = forward(lanes(parts), first_ref, inner_ref, twist_ref)
    vspec_ref[...] = vspec
    spectra = []
    for b in range(DP):
        v_real, v_imag = vspec[b * HALF:(b + 1) * HALF, :LANES], vspec[b * HALF:(b + 1) * HALF, LANES:]
        spectra.append(lanes([v_real * f_real - v_imag * f_imag, v_real * f_imag + v_imag * f_real]))
    conv = table_dot(inv_ref, *inverse_inner(rows(spectra), inner_t_ref, twist_ref))
    for b in range(DP):
        conv_ref[b * size:(b + 1) * size, :] = conv[:, b * LANES:(b + 1) * LANES].astype(BF16)


def partial_grads(cot_ref, *refs):
    *refs, buffer, sems = refs
    count = len(refs) // 2
    copies = [
        pltpu.make_async_copy(cot_ref.at[pl.ds(k * HALVES, HALVES)], buffer.at[pl.ds(k * HALVES, HALVES)], sems.at[k])
        for k in range(2)
    ]
    for copy in copies:
        copy.start()
    columns = rows([ref[...] for ref in refs[:count]])
    for k, copy in enumerate(copies):
        block = slice(k * HALVES, (k + 1) * HALVES)
        copy.wait()
        out = lax.dot_general(
            buffer[block, :], columns, (((1,), (1,)), ((), ())), preferred_element_type=F32
        ).astype(BF16)
        for group, ref in enumerate(refs[count:]):
            ref[block, :] = out[:, group * LANES:(group + 1) * LANES]


def pack_grads(*refs):
    query_ref, conv_ref, spread_ref = refs[:3]
    pieces, (out_ref, grad_ref) = refs[3:-2], refs[-2:]
    grad = pieces[0][...].astype(F32)
    for piece in pieces[1:]:
        grad = grad + piece[...].astype(F32)
    grad_ref[...] = grad
    grad_conv = grad * query_ref[...].astype(F32)
    tiles = [grad_conv[q * LANES:(q + 1) * LANES, :].T.astype(BF16) for q in range(ROWS)]
    spread = spread_ref[:, 128:]
    for part in range(4):
        block = jnp.concatenate([tile[part * 32:(part + 1) * 32] for tile in tiles], axis=0)
        out_ref[part * 256:(part + 1) * 256, :] = (
            dot(spread, block) + conv_ref[part * 256:(part + 1) * 256, :].astype(F32)
        ).astype(BF16)


def gather_half(got_ref, gather):
    blocks = [dot(gather, got_ref[part * 256:(part + 1) * 256, :]) for part in range(4)]
    return [
        jnp.concatenate([block[q * 32:(q + 1) * 32] for block in blocks], axis=0).T for q in range(gather.shape[0] // 32)
    ]


def unpack_conv(got_ref, query_ref, grad_ref, gather_ref, gated_ref, grad_query_ref):
    for q, conv in enumerate(gather_half(got_ref, gather_ref[:128, :])):
        cut = slice(q * LANES, (q + 1) * LANES)
        gated_ref[cut, :] = (query_ref[cut, :].astype(F32) * conv).astype(BF16)
        grad_query_ref[cut, :] = (grad_ref[cut, :] * conv).astype(BF16)


def correlate(
    got_ref, vspec_ref, fspec_ref, second_ref, inv_first_ref, inv_second_ref, inner_ref, inner_t_ref, twist_ref, out_ref
):
    size = SEQ * SLOTS
    f_real, f_imag = fspec_ref[:, :LANES], fspec_ref[:, LANES:]
    sum_real = sum_imag = None
    spec = forward(
        lanes([got_ref[b * size:(b + 1) * size, :] for b in range(DP)]), second_ref, inner_ref, twist_ref
    )
    spectra = []
    for b in range(DP):
        block = slice(b * HALF, (b + 1) * HALF)
        real, imag = spec[block, :LANES], spec[block, LANES:]
        v_real, v_imag = vspec_ref[block, :LANES], vspec_ref[block, LANES:]
        part_real = real * v_real + imag * v_imag
        part_imag = imag * v_real - real * v_imag
        sum_real = part_real if b == 0 else sum_real + part_real
        sum_imag = part_imag if b == 0 else sum_imag + part_imag
        spectra.append(lanes([real * f_real + imag * f_imag, imag * f_real - real * f_imag]))
    spectra.append(lanes([sum_real, sum_imag]))
    high, low = inverse_inner(rows(spectra), inner_t_ref, twist_ref)
    cut = DP * LANES
    value = table_dot(inv_first_ref, high[:, :cut], low[:, :cut])
    filt = table_dot(inv_second_ref, high[:, cut:], low[:, cut:])
    for b in range(DP):
        out_ref[b * size:(b + 1) * size, :] = (value[:, b * LANES:(b + 1) * LANES] + filt).astype(BF16)


def unpack_grads(got_ref, gather_ref, value_ref, filt_ref):
    tiles = gather_half(got_ref, gather_ref[...])
    for q in range(ROWS):
        value_ref[q * LANES:(q + 1) * LANES, :] = tiles[q].astype(BF16)
        filt_ref[q * LANES:(q + 1) * LANES, :] = tiles[ROWS + q]


def project(gated_ref, *refs):
    *refs, out_ref, buffer, sems = refs
    count = len(refs)
    length = buffer.shape[0]
    rank = lax.axis_index("tensor")
    starts = [pl.multiple_of((rank + count - d) % count * length, length) for d in range(count)]
    gated = lanes([gated_ref[pl.ds(start, length), :] for start in starts])
    copies = []
    for k in range(buffer.shape[1] // CHUNK):
        cut = slice(k * CHUNK, (k + 1) * CHUNK)
        buffer[:, cut] = dot(gated, rows([ref[:, cut] for ref in refs])).astype(BF16)
        cut = pl.ds(k * CHUNK, CHUNK)
        copies.append(pltpu.make_async_copy(buffer.at[:, cut], out_ref.at[:, cut], sems.at[k]))
        copies[-1].start()
    for copy in copies:
        copy.wait()


COVER = pl.CostEstimate(flops=40_000_000_000, transcendentals=0, bytes_accessed=40_000_000)
COVERS = {"pack_inputs": COVER, "partial_grads": COVER}


def call(kernel, outs, *operands, **options):
    return pl.pallas_call(
        kernel,
        out_shape=outs,
        **options,
        name=kernel.__name__,
        cost_estimate=COVERS.get(kernel.__name__),
        compiler_params=pltpu.CompilerParams(vmem_limit_bytes=40 * 1024 * 1024),
    )(*operands)


def exchange(message, turn=0):
    shape = message.shape
    message = message.reshape(DP * SEQ, SLOTS, LANES)
    group = [b * SEQ + (s + turn) % SEQ for b in range(DP) for s in range(SEQ)]
    return lax.all_to_all(
        message, ("dp", "seq"), split_axis=0, concat_axis=0, tiled=True, axis_index_groups=[group] if turn else None
    ).reshape(shape)


def shifted(array, distance, count):
    return lax.ppermute(array, "tensor", [(i, (i + distance) % count) for i in range(count)])


def per_device(queries, values, filt, w_out, cotangent, count):
    t = tables()
    query = queries[0]
    length, width = query.shape
    features = cotangent.shape[2]
    rank = lax.axis_index("tensor")
    vmem = pl.BlockSpec(memory_space=pltpu.VMEM)
    message = jax.ShapeDtypeStruct((DP * SEQ * SLOTS, LANES), BF16)
    signal = jax.ShapeDtypeStruct((length, width), BF16)

    columns = []
    for d in range(count):
        piece = lax.dynamic_slice(w_out, (0, (rank + d) % count * features), (width, features))
        columns.append(shifted(piece, d, count) if d else piece)

    got = exchange(call(pack_inputs, message, values[0], filt, t["turned_spread"]), TURN)
    conv, value_spec, filt_spec = call(
        convolve,
        [
            message,
            jax.ShapeDtypeStruct((DP * HALF, 2 * LANES), F32),
            jax.ShapeDtypeStruct((HALF, 2 * LANES), F32),
        ],
        got, t["turned_first"], t["turned_second"], t["inv_first"], t["inner"], t["inner_t"], t["twist"],
    )
    partial = call(
        partial_grads, [signal] * count, pltpu.with_memory_space_constraint(cotangent[0], pltpu.HBM), *columns,
        in_specs=[pl.BlockSpec(memory_space=pltpu.HBM)] + [vmem] * count,
        scratch_shapes=[pltpu.VMEM((length, features), BF16), pltpu.SemaphoreType.DMA((2,))],
    )
    partial = [shifted(p, -d, count) if d else p for d, p in enumerate(partial)]
    outgoing, grad_gated = call(
        pack_grads, [message, jax.ShapeDtypeStruct((length, width), F32)], query, conv, t["spread"], *partial
    )
    got = exchange(outgoing)
    gated, grad_query = call(unpack_conv, [signal, signal], got, query, grad_gated, t["spread"].T)
    gathered = lax.all_gather(gated, "tensor", axis=0, tiled=True)
    got = exchange(
        call(
            correlate, message, got, value_spec, filt_spec, t["fwd_second"], t["inv_first"], t["inv_second"],
            t["inner"], t["inner_t"], t["twist"],
        )
    )
    mixed = call(
        project, jax.ShapeDtypeStruct((length, features), BF16), gathered, *columns,
        out_specs=pl.BlockSpec(memory_space=pltpu.HBM),
        scratch_shapes=[pltpu.VMEM((length, features), BF16), pltpu.SemaphoreType.DMA((features // CHUNK,))],
    )
    grad_value, grad_filt = call(
        unpack_grads, [signal, jax.ShapeDtypeStruct((length, width), F32)], got, t["spread"].T
    )
    return (mixed[None], grad_query[None], grad_value[None], grad_filt)


def solution(mesh):
    placed = (
        P("dp", "seq", "tensor"),
        P("dp", "seq", "tensor"),
        P("seq", "tensor"),
        P("tensor", None),
        P("dp", "seq", "tensor"),
    )
    return jax.shard_map(
        functools.partial(per_device, count=mesh.shape["tensor"]),
        mesh=mesh,
        in_specs=placed,
        out_specs=(
            P("dp", "seq", "tensor"),
            P("dp", "seq", "tensor"),
            P("dp", "seq", "tensor"),
            P("seq", "tensor"),
        ),
        check_vma=False,
    )
```

```python
import functools
import math

import jax
import jax.numpy as jnp
import ml_dtypes
import numpy as np
from jax import lax
from jax.experimental import pallas as pl
from jax.experimental.pallas import tpu as pltpu
from jax.sharding import PartitionSpec as P

F32 = jnp.float32
BF16 = jnp.bfloat16
DP = 4
SEQ = 32
ROWS = 4
LANES = 128
CHUNK = 256
HALVES = 256
SLOTS = 8
TURN = 22
HALF = 128


def narrow(table):
    return table.astype(ml_dtypes.bfloat16)


@functools.cache
def tables():
    coarse = np.arange(HALF) + 0.5
    row = np.arange(SEQ * SLOTS)

    def outer(turn):
        place = (row // SLOTS + turn) % SEQ * ROWS + row % SLOTS % ROWS
        angle = 2 * math.pi / 256 * coarse[:, None] * place[None, :]
        full = np.concatenate([np.cos(angle), -np.sin(angle)])
        first = np.where(row[None, :] % SLOTS < ROWS, full, 0.0)
        return first, full - first

    first, second = outer(0)
    turned_first, turned_second = outer(TURN)
    fine = np.arange(LANES)
    angle = 2 * math.pi / LANES * np.outer(fine, fine)
    cos, sin = np.cos(angle), np.sin(angle)
    inner = np.block([[cos, -sin], [sin, cos]])
    angle = 2 * math.pi / 32768 * np.outer(coarse, fine)
    twist = np.stack([np.cos(angle), np.sin(angle)]).astype(np.float32)
    spread, turned_spread = np.zeros((256, 256)), np.zeros((256, 256))
    for channel in range(32):
        for slot in range(SLOTS):
            spread[channel * SLOTS + slot, slot * 32 + channel] = 1.0
            turned_spread[channel * SLOTS + slot, slot * 32 + (channel + TURN) % 32] = 1.0
    return {
        "turned_first": narrow(turned_first),
        "turned_second": narrow(turned_second),
        "fwd_second": narrow(second),
        "inv_first": narrow(first.T / 16384),
        "inv_second": narrow(second.T / 16384),
        "inner": narrow(inner),
        "inner_t": narrow(inner.T),
        "twist": twist,
        "spread": narrow(spread),
        "turned_spread": narrow(turned_spread),
    }


def dot(left, right):
    return jnp.dot(left, right, preferred_element_type=F32)


def lanes(tiles):
    return jnp.concatenate(tiles, axis=1)


def rows(tiles):
    return jnp.concatenate(tiles, axis=0)


def forward(signals, outer_ref, inner_ref, twist_ref):
    count = signals.shape[1] // LANES
    coarse = dot(outer_ref[...], signals)
    cos, sin = lanes([twist_ref[0]] * count), lanes([twist_ref[1]] * count)
    real, imag = coarse[:HALF], coarse[HALF:]
    real, imag = real * cos + imag * sin, imag * cos - real * sin
    cuts = [slice(k * LANES, (k + 1) * LANES) for k in range(count)]
    return dot(rows([lanes([real[:, cut], imag[:, cut]]) for cut in cuts]).astype(BF16), inner_ref[...])


def inverse_inner(spectra, inner_t_ref, twist_ref):
    count = spectra.shape[0] // HALF
    coarse = dot(spectra.astype(BF16), inner_t_ref[...])
    cos, sin = twist_ref[0], twist_ref[1]
    out = []
    for k in range(count):
        real, imag = coarse[k * HALF:(k + 1) * HALF, :LANES], coarse[k * HALF:(k + 1) * HALF, LANES:]
        out.append(rows([real * cos - imag * sin, imag * cos + real * sin]))
    return lanes(out).astype(BF16)


def pack_inputs(values_ref, filt_ref, spread_ref, out_ref):
    dp = lax.axis_index("dp")
    start = pl.multiple_of(dp * LANES, LANES)
    quarter = filt_ref[pl.ds(start, LANES), :].T
    tiles = [values_ref[q * LANES:(q + 1) * LANES, :].astype(F32).T.astype(BF16) for q in range(ROWS)]
    tiles += [jnp.where(dp == q, quarter, 0.0).astype(BF16) for q in range(DP)]
    for part in range(4):
        block = jnp.concatenate([tile[part * 32:(part + 1) * 32] for tile in tiles], axis=0)
        out_ref[part * 256:(part + 1) * 256, :] = dot(spread_ref[...], block).astype(BF16)


def convolve(got_ref, first_ref, second_ref, inv_ref, inner_ref, inner_t_ref, twist_ref, conv_ref, vspec_ref, fspec_ref):
    size = SEQ * SLOTS
    parts = [got_ref[b * size:(b + 1) * size, :] for b in range(DP)]
    filt = ((parts[0].astype(F32) + parts[1].astype(F32)) + (parts[2].astype(F32) + parts[3].astype(F32))).astype(BF16)
    fspec = forward(filt, second_ref, inner_ref, twist_ref)
    fspec_ref[...] = fspec
    f_real, f_imag = fspec[:, :LANES], fspec[:, LANES:]
    vspec = forward(lanes(parts), first_ref, inner_ref, twist_ref)
    vspec_ref[...] = vspec
    spectra = []
    for b in range(DP):
        v_real, v_imag = vspec[b * HALF:(b + 1) * HALF, :LANES], vspec[b * HALF:(b + 1) * HALF, LANES:]
        spectra.append(lanes([v_real * f_real - v_imag * f_imag, v_real * f_imag + v_imag * f_real]))
    conv = dot(inv_ref[...], inverse_inner(rows(spectra), inner_t_ref, twist_ref))
    for b in range(DP):
        conv_ref[b * size:(b + 1) * size, :] = conv[:, b * LANES:(b + 1) * LANES].astype(BF16)


def partial_grads(cot_ref, *refs):
    *refs, buffer, sems = refs
    count = len(refs) // 2
    copies = [
        pltpu.make_async_copy(cot_ref.at[pl.ds(k * HALVES, HALVES)], buffer.at[pl.ds(k * HALVES, HALVES)], sems.at[k])
        for k in range(2)
    ]
    for copy in copies:
        copy.start()
    columns = rows([ref[...] for ref in refs[:count]])
    for k, copy in enumerate(copies):
        block = slice(k * HALVES, (k + 1) * HALVES)
        copy.wait()
        out = lax.dot_general(
            buffer[block, :], columns, (((1,), (1,)), ((), ())), preferred_element_type=F32
        ).astype(BF16)
        for group, ref in enumerate(refs[count:]):
            ref[block, :] = out[:, group * LANES:(group + 1) * LANES]


def pack_grads(*refs):
    query_ref, conv_ref, spread_ref = refs[:3]
    pieces, (out_ref, grad_ref) = refs[3:-2], refs[-2:]
    grad = pieces[0][...].astype(F32)
    for piece in pieces[1:]:
        grad = grad + piece[...].astype(F32)
    grad_ref[...] = grad
    grad_conv = grad * query_ref[...].astype(F32)
    tiles = [grad_conv[q * LANES:(q + 1) * LANES, :].T.astype(BF16) for q in range(ROWS)]
    spread = spread_ref[:, 128:]
    for part in range(4):
        block = jnp.concatenate([tile[part * 32:(part + 1) * 32] for tile in tiles], axis=0)
        out_ref[part * 256:(part + 1) * 256, :] = (
            dot(spread, block) + conv_ref[part * 256:(part + 1) * 256, :].astype(F32)
        ).astype(BF16)


def gather_half(got_ref, gather):
    blocks = [dot(gather, got_ref[part * 256:(part + 1) * 256, :]) for part in range(4)]
    return [
        jnp.concatenate([block[q * 32:(q + 1) * 32] for block in blocks], axis=0).T for q in range(gather.shape[0] // 32)
    ]


def unpack_conv(got_ref, query_ref, grad_ref, gather_ref, gated_ref, grad_query_ref):
    for q, conv in enumerate(gather_half(got_ref, gather_ref[:128, :])):
        cut = slice(q * LANES, (q + 1) * LANES)
        gated_ref[cut, :] = (query_ref[cut, :].astype(F32) * conv).astype(BF16)
        grad_query_ref[cut, :] = (grad_ref[cut, :] * conv).astype(BF16)


def correlate(
    got_ref, vspec_ref, fspec_ref, second_ref, inv_first_ref, inv_second_ref, inner_ref, inner_t_ref, twist_ref, out_ref
):
    size = SEQ * SLOTS
    f_real, f_imag = fspec_ref[:, :LANES], fspec_ref[:, LANES:]
    sum_real = sum_imag = None
    spec = forward(
        lanes([got_ref[b * size:(b + 1) * size, :] for b in range(DP)]), second_ref, inner_ref, twist_ref
    )
    spectra = []
    for b in range(DP):
        block = slice(b * HALF, (b + 1) * HALF)
        real, imag = spec[block, :LANES], spec[block, LANES:]
        v_real, v_imag = vspec_ref[block, :LANES], vspec_ref[block, LANES:]
        part_real = real * v_real + imag * v_imag
        part_imag = imag * v_real - real * v_imag
        sum_real = part_real if b == 0 else sum_real + part_real
        sum_imag = part_imag if b == 0 else sum_imag + part_imag
        spectra.append(lanes([real * f_real + imag * f_imag, imag * f_real - real * f_imag]))
    spectra.append(lanes([sum_real, sum_imag]))
    coarse = inverse_inner(rows(spectra), inner_t_ref, twist_ref)
    cut = DP * LANES
    value = dot(inv_first_ref[...], coarse[:, :cut])
    filt = dot(inv_second_ref[...], coarse[:, cut:])
    for b in range(DP):
        out_ref[b * size:(b + 1) * size, :] = (value[:, b * LANES:(b + 1) * LANES] + filt).astype(BF16)


def finish(gated_ref, *refs):
    *refs, got_ref, gather_ref, mixed_ref, value_ref, filt_ref, mixed, value, filt, sems = refs
    count = len(refs)
    length = mixed.shape[0]
    rank = lax.axis_index("tensor")
    starts = [pl.multiple_of((rank + count - d) % count * length, length) for d in range(count)]
    gated = lanes([gated_ref[pl.ds(start, length), :] for start in starts])
    copies = []

    def send(buffer, ref, index):
        copies.append(pltpu.make_async_copy(buffer.at[index], ref.at[index], sems.at[len(copies)]))
        copies[-1].start()

    for k in range(mixed.shape[1] // CHUNK):
        cut = slice(k * CHUNK, (k + 1) * CHUNK)
        mixed[:, cut] = dot(gated, rows([ref[:, cut] for ref in refs])).astype(BF16)
        send(mixed, mixed_ref, (slice(None), pl.ds(k * CHUNK, CHUNK)))
    tiles = gather_half(got_ref, gather_ref[...])
    for q in range(ROWS):
        cut = slice(q * LANES, (q + 1) * LANES)
        value[cut, :] = tiles[q].astype(BF16)
        filt[cut, :] = tiles[ROWS + q]
    everything = (pl.ds(0, length), slice(None))
    send(value, value_ref, everything)
    send(filt, filt_ref, everything)
    for copy in copies:
        copy.wait()


COVER = pl.CostEstimate(flops=40_000_000_000, transcendentals=0, bytes_accessed=40_000_000)
COVERS = {"pack_inputs": COVER, "partial_grads": COVER}


def call(kernel, outs, *operands, **options):
    return pl.pallas_call(
        kernel,
        out_shape=outs,
        **options,
        name=kernel.__name__,
        cost_estimate=COVERS.get(kernel.__name__),
        compiler_params=pltpu.CompilerParams(vmem_limit_bytes=40 * 1024 * 1024),
    )(*operands)


def exchange(message, turn=0):
    shape = message.shape
    message = message.reshape(DP * SEQ, SLOTS, LANES)
    group = [b * SEQ + (s + turn) % SEQ for b in range(DP) for s in range(SEQ)]
    return lax.all_to_all(
        message, ("dp", "seq"), split_axis=0, concat_axis=0, tiled=True, axis_index_groups=[group] if turn else None
    ).reshape(shape)


def shifted(array, distance, count):
    return lax.ppermute(array, "tensor", [(i, (i + distance) % count) for i in range(count)])


def per_device(queries, values, filt, w_out, cotangent, count):
    t = tables()
    query = queries[0]
    length, width = query.shape
    features = cotangent.shape[2]
    rank = lax.axis_index("tensor")
    vmem = pl.BlockSpec(memory_space=pltpu.VMEM)
    message = jax.ShapeDtypeStruct((DP * SEQ * SLOTS, LANES), BF16)
    signal = jax.ShapeDtypeStruct((length, width), BF16)

    columns = []
    for d in range(count):
        piece = lax.dynamic_slice(w_out, (0, (rank + d) % count * features), (width, features))
        columns.append(shifted(piece, d, count) if d else piece)

    got = exchange(call(pack_inputs, message, values[0], filt, t["turned_spread"]), TURN)
    conv, value_spec, filt_spec = call(
        convolve,
        [
            message,
            jax.ShapeDtypeStruct((DP * HALF, 2 * LANES), F32),
            jax.ShapeDtypeStruct((HALF, 2 * LANES), F32),
        ],
        got, t["turned_first"], t["turned_second"], t["inv_first"], t["inner"], t["inner_t"], t["twist"],
    )
    partial = call(
        partial_grads, [signal] * count, pltpu.with_memory_space_constraint(cotangent[0], pltpu.HBM), *columns,
        in_specs=[pl.BlockSpec(memory_space=pltpu.HBM)] + [vmem] * count,
        scratch_shapes=[pltpu.VMEM((length, features), BF16), pltpu.SemaphoreType.DMA((2,))],
    )
    partial = [shifted(p, -d, count) if d else p for d, p in enumerate(partial)]
    outgoing, grad_gated = call(
        pack_grads, [message, jax.ShapeDtypeStruct((length, width), F32)], query, conv, t["spread"], *partial
    )
    got = exchange(outgoing)
    gated, grad_query = call(unpack_conv, [signal, signal], got, query, grad_gated, t["spread"].T)
    gathered = lax.all_gather(gated, "tensor", axis=0, tiled=True)
    got = exchange(
        call(
            correlate, message, got, value_spec, filt_spec, t["fwd_second"], t["inv_first"], t["inv_second"],
            t["inner"], t["inner_t"], t["twist"],
        )
    )
    wide = (length, features)
    mixed, grad_value, grad_filt = call(
        finish,
        [jax.ShapeDtypeStruct(wide, BF16), signal, jax.ShapeDtypeStruct((length, width), F32)],
        gathered, *columns, got, t["spread"].T,
        out_specs=[pl.BlockSpec(memory_space=pltpu.HBM)] * 3,
        scratch_shapes=[
            pltpu.VMEM(wide, BF16),
            pltpu.VMEM((length, width), BF16),
            pltpu.VMEM((length, width), F32),
            pltpu.SemaphoreType.DMA((features // CHUNK + 2,)),
        ],
    )
    return (mixed[None], grad_query[None], grad_value[None], grad_filt)


def solution(mesh):
    placed = (
        P("dp", "seq", "tensor"),
        P("dp", "seq", "tensor"),
        P("seq", "tensor"),
        P("tensor", None),
        P("dp", "seq", "tensor"),
    )
    return jax.shard_map(
        functools.partial(per_device, count=mesh.shape["tensor"]),
        mesh=mesh,
        in_specs=placed,
        out_specs=(
            P("dp", "seq", "tensor"),
            P("dp", "seq", "tensor"),
            P("dp", "seq", "tensor"),
            P("seq", "tensor"),
        ),
        check_vma=False,
    )
```

```python
import functools
import math

import jax
import jax.numpy as jnp
import ml_dtypes
import numpy as np
from jax import lax
from jax.experimental import pallas as pl
from jax.experimental.pallas import tpu as pltpu
from jax.sharding import PartitionSpec as P

F32 = jnp.float32
BF16 = jnp.bfloat16
DP = 4
SEQ = 32
ROWS = 4
LANES = 128
CHUNK = 256
HALVES = 256
SLOTS = 8
TURN = 22
LATER = 0
HALF = 128


def narrow(table):
    return table.astype(ml_dtypes.bfloat16)


@functools.cache
def tables():
    coarse = np.arange(HALF) + 0.5
    row = np.arange(SEQ * SLOTS)

    def outer(turn):
        place = (row // SLOTS + turn) % SEQ * ROWS + row % SLOTS % ROWS
        angle = 2 * math.pi / 256 * coarse[:, None] * place[None, :]
        full = np.concatenate([np.cos(angle), -np.sin(angle)])
        first = np.where(row[None, :] % SLOTS < ROWS, full, 0.0)
        return first, full - first

    first, second = outer(LATER)
    turned_first, turned_second = outer(TURN)
    fine = np.arange(LANES)
    angle = 2 * math.pi / LANES * np.outer(fine, fine)
    cos, sin = np.cos(angle), np.sin(angle)
    inner = np.block([[cos, -sin], [sin, cos]])
    angle = 2 * math.pi / 32768 * np.outer(coarse, fine)
    twist = np.stack([np.cos(angle), np.sin(angle)]).astype(np.float32)
    spread, turned_spread = np.zeros((256, 256)), np.zeros((256, 256))
    for channel in range(32):
        for slot in range(SLOTS):
            spread[channel * SLOTS + slot, slot * 32 + channel] = 1.0
            turned_spread[channel * SLOTS + slot, slot * 32 + (channel + TURN - LATER) % 32] = 1.0
    return {
        "turned_first": narrow(turned_first),
        "turned_second": narrow(turned_second),
        "fwd_second": narrow(second),
        "inv_first": narrow(first.T / 16384),
        "inv_second": narrow(second.T / 16384),
        "inner": narrow(inner),
        "inner_t": narrow(inner.T),
        "twist": twist,
        "spread": narrow(spread),
        "turned_spread": narrow(turned_spread),
    }


def dot(left, right):
    return jnp.dot(left, right, preferred_element_type=F32)


def lanes(tiles):
    return jnp.concatenate(tiles, axis=1)


def rows(tiles):
    return jnp.concatenate(tiles, axis=0)


def forward(signals, outer_ref, inner_ref, twist_ref):
    count = signals.shape[1] // LANES
    coarse = dot(outer_ref[...], signals)
    cos, sin = lanes([twist_ref[0]] * count), lanes([twist_ref[1]] * count)
    real, imag = coarse[:HALF], coarse[HALF:]
    real, imag = real * cos + imag * sin, imag * cos - real * sin
    cuts = [slice(k * LANES, (k + 1) * LANES) for k in range(count)]
    return dot(rows([lanes([real[:, cut], imag[:, cut]]) for cut in cuts]).astype(BF16), inner_ref[...])


def inverse_inner(spectra, inner_t_ref, twist_ref):
    count = spectra.shape[0] // HALF
    coarse = dot(spectra.astype(BF16), inner_t_ref[...])
    cos, sin = twist_ref[0], twist_ref[1]
    out = []
    for k in range(count):
        real, imag = coarse[k * HALF:(k + 1) * HALF, :LANES], coarse[k * HALF:(k + 1) * HALF, LANES:]
        out.append(rows([real * cos - imag * sin, imag * cos + real * sin]))
    return lanes(out).astype(BF16)


def pack_inputs(values_ref, filt_ref, spread_ref, out_ref):
    dp = lax.axis_index("dp")
    start = pl.multiple_of(dp * LANES, LANES)
    quarter = filt_ref[pl.ds(start, LANES), :].T
    tiles = [values_ref[q * LANES:(q + 1) * LANES, :].T for q in range(ROWS)]
    tiles += [jnp.where(dp == q, quarter, 0.0).astype(BF16) for q in range(DP)]
    for part in range(4):
        block = jnp.concatenate([tile[part * 32:(part + 1) * 32] for tile in tiles], axis=0)
        out_ref[part * 256:(part + 1) * 256, :] = dot(spread_ref[...], block).astype(BF16)


def convolve(got_ref, first_ref, second_ref, inv_ref, inner_ref, inner_t_ref, twist_ref, conv_ref, vspec_ref, fspec_ref):
    size = SEQ * SLOTS
    parts = [got_ref[b * size:(b + 1) * size, :] for b in range(DP)]
    filt = ((parts[0].astype(F32) + parts[1].astype(F32)) + (parts[2].astype(F32) + parts[3].astype(F32))).astype(BF16)
    fspec = forward(filt, second_ref, inner_ref, twist_ref)
    fspec_ref[...] = fspec
    f_real, f_imag = fspec[:, :LANES], fspec[:, LANES:]
    vspec = forward(lanes(parts), first_ref, inner_ref, twist_ref)
    vspec_ref[...] = vspec
    spectra = []
    for b in range(DP):
        v_real, v_imag = vspec[b * HALF:(b + 1) * HALF, :LANES], vspec[b * HALF:(b + 1) * HALF, LANES:]
        spectra.append(lanes([v_real * f_real - v_imag * f_imag, v_real * f_imag + v_imag * f_real]))
    conv = dot(inv_ref[...], inverse_inner(rows(spectra), inner_t_ref, twist_ref))
    for b in range(DP):
        conv_ref[b * size:(b + 1) * size, :] = conv[:, b * LANES:(b + 1) * LANES].astype(BF16)


def partial_grads(cot_ref, *refs):
    *refs, buffer, sems = refs
    count = len(refs) // 2
    copies = [
        pltpu.make_async_copy(cot_ref.at[pl.ds(k * HALVES, HALVES)], buffer.at[pl.ds(k * HALVES, HALVES)], sems.at[k])
        for k in range(2)
    ]
    for copy in copies:
        copy.start()
    columns = rows([ref[...] for ref in refs[:count]])
    for k, copy in enumerate(copies):
        block = slice(k * HALVES, (k + 1) * HALVES)
        copy.wait()
        out = lax.dot_general(
            buffer[block, :], columns, (((1,), (1,)), ((), ())), preferred_element_type=F32
        ).astype(BF16)
        for group, ref in enumerate(refs[count:]):
            ref[block, :] = out[:, group * LANES:(group + 1) * LANES]


def pack_grads(*refs):
    query_ref, conv_ref, spread_ref = refs[:3]
    pieces, (out_ref, grad_ref) = refs[3:-2], refs[-2:]
    grad = pieces[0][...].astype(F32)
    for piece in pieces[1:]:
        grad = grad + piece[...].astype(F32)
    grad_ref[...] = grad
    grad_conv = grad * query_ref[...].astype(F32)
    tiles = [grad_conv[q * LANES:(q + 1) * LANES, :].T.astype(BF16) for q in range(ROWS)]
    spread = spread_ref[:, 128:]
    for part in range(4):
        block = jnp.concatenate([tile[part * 32:(part + 1) * 32] for tile in tiles], axis=0)
        out_ref[part * 256:(part + 1) * 256, :] = (
            dot(spread, block) + conv_ref[part * 256:(part + 1) * 256, :].astype(F32)
        ).astype(BF16)


def gather_half(got_ref, gather):
    blocks = [dot(gather, got_ref[part * 256:(part + 1) * 256, :]) for part in range(4)]
    return [
        jnp.concatenate([block[q * 32:(q + 1) * 32] for block in blocks], axis=0).T for q in range(gather.shape[0] // 32)
    ]


def unpack_conv(got_ref, query_ref, grad_ref, gather_ref, gated_ref, grad_query_ref):
    for q, conv in enumerate(gather_half(got_ref, gather_ref[:128, :])):
        cut = slice(q * LANES, (q + 1) * LANES)
        gated_ref[cut, :] = (query_ref[cut, :].astype(F32) * conv).astype(BF16)
        grad_query_ref[cut, :] = (grad_ref[cut, :] * conv).astype(BF16)


def correlate(
    got_ref, vspec_ref, fspec_ref, second_ref, inv_first_ref, inv_second_ref, inner_ref, inner_t_ref, twist_ref, out_ref
):
    size = SEQ * SLOTS
    f_real, f_imag = fspec_ref[:, :LANES], fspec_ref[:, LANES:]
    sum_real = sum_imag = None
    spec = forward(
        lanes([got_ref[b * size:(b + 1) * size, :] for b in range(DP)]), second_ref, inner_ref, twist_ref
    )
    spectra = []
    for b in range(DP):
        block = slice(b * HALF, (b + 1) * HALF)
        real, imag = spec[block, :LANES], spec[block, LANES:]
        v_real, v_imag = vspec_ref[block, :LANES], vspec_ref[block, LANES:]
        part_real = real * v_real + imag * v_imag
        part_imag = imag * v_real - real * v_imag
        sum_real = part_real if b == 0 else sum_real + part_real
        sum_imag = part_imag if b == 0 else sum_imag + part_imag
        spectra.append(lanes([real * f_real + imag * f_imag, imag * f_real - real * f_imag]))
    spectra.append(lanes([sum_real, sum_imag]))
    coarse = inverse_inner(rows(spectra), inner_t_ref, twist_ref)
    cut = DP * LANES
    value = dot(inv_first_ref[...], coarse[:, :cut])
    filt = dot(inv_second_ref[...], coarse[:, cut:])
    for b in range(DP):
        out_ref[b * size:(b + 1) * size, :] = (value[:, b * LANES:(b + 1) * LANES] + filt).astype(BF16)


def project(gated_ref, *refs):
    *refs, out_ref, buffer, sems = refs
    count = len(refs)
    length = buffer.shape[0]
    rank = lax.axis_index("tensor")
    starts = [pl.multiple_of((rank + count - d) % count * length, length) for d in range(count)]
    gated = lanes([gated_ref[pl.ds(start, length), :] for start in starts])
    copies = []
    for k in range(buffer.shape[1] // CHUNK):
        cut = slice(k * CHUNK, (k + 1) * CHUNK)
        buffer[:, cut] = dot(gated, rows([ref[:, cut] for ref in refs])).astype(BF16)
        cut = pl.ds(k * CHUNK, CHUNK)
        copies.append(pltpu.make_async_copy(buffer.at[:, cut], out_ref.at[:, cut], sems.at[k]))
        copies[-1].start()
    for copy in copies:
        copy.wait()


def unpack_grads(got_ref, gather_ref, value_ref, filt_ref):
    tiles = gather_half(got_ref, gather_ref[...])
    for q in range(ROWS):
        value_ref[q * LANES:(q + 1) * LANES, :] = tiles[q].astype(BF16)
        filt_ref[q * LANES:(q + 1) * LANES, :] = tiles[ROWS + q]


COVER = pl.CostEstimate(flops=40_000_000_000, transcendentals=0, bytes_accessed=40_000_000)
COVERS = {"pack_inputs": COVER, "partial_grads": COVER}


def call(kernel, outs, *operands, **options):
    return pl.pallas_call(
        kernel,
        out_shape=outs,
        **options,
        name=kernel.__name__,
        cost_estimate=COVERS.get(kernel.__name__),
        compiler_params=pltpu.CompilerParams(vmem_limit_bytes=40 * 1024 * 1024),
    )(*operands)


def exchange(message, turn=LATER):
    shape = message.shape
    message = message.reshape(DP * SEQ, SLOTS, LANES)
    group = [b * SEQ + (s + turn) % SEQ for b in range(DP) for s in range(SEQ)]
    return lax.all_to_all(
        message, ("dp", "seq"), split_axis=0, concat_axis=0, tiled=True, axis_index_groups=[group] if turn else None
    ).reshape(shape)


def shifted(array, distance, count):
    return lax.ppermute(array, "tensor", [(i, (i + distance) % count) for i in range(count)])


def per_device(queries, values, filt, w_out, cotangent, count):
    t = tables()
    query = queries[0]
    length, width = query.shape
    features = cotangent.shape[2]
    rank = lax.axis_index("tensor")
    vmem = pl.BlockSpec(memory_space=pltpu.VMEM)
    message = jax.ShapeDtypeStruct((DP * SEQ * SLOTS, LANES), BF16)
    signal = jax.ShapeDtypeStruct((length, width), BF16)

    columns = []
    for d in range(count):
        piece = lax.dynamic_slice(w_out, (0, (rank + d) % count * features), (width, features))
        columns.append(shifted(piece, d, count) if d else piece)

    got = exchange(call(pack_inputs, message, values[0], filt, t["turned_spread"]), TURN)
    conv, value_spec, filt_spec = call(
        convolve,
        [
            message,
            jax.ShapeDtypeStruct((DP * HALF, 2 * LANES), F32),
            jax.ShapeDtypeStruct((HALF, 2 * LANES), F32),
        ],
        got, t["turned_first"], t["turned_second"], t["inv_first"], t["inner"], t["inner_t"], t["twist"],
    )
    partial = call(
        partial_grads, [signal] * count, pltpu.with_memory_space_constraint(cotangent[0], pltpu.HBM), *columns,
        in_specs=[pl.BlockSpec(memory_space=pltpu.HBM)] + [vmem] * count,
        scratch_shapes=[pltpu.VMEM((length, features), BF16), pltpu.SemaphoreType.DMA((2,))],
    )
    partial = [shifted(p, -d, count) if d else p for d, p in enumerate(partial)]
    outgoing, grad_gated = call(
        pack_grads, [message, jax.ShapeDtypeStruct((length, width), F32)], query, conv, t["spread"], *partial
    )
    got = exchange(outgoing)
    gated, grad_query = call(unpack_conv, [signal, signal], got, query, grad_gated, t["spread"].T)
    gathered = lax.all_gather(gated, "tensor", axis=0, tiled=True)
    got = exchange(
        call(
            correlate, message, got, value_spec, filt_spec, t["fwd_second"], t["inv_first"], t["inv_second"],
            t["inner"], t["inner_t"], t["twist"],
        )
    )
    mixed = call(
        project, jax.ShapeDtypeStruct((length, features), BF16), gathered, *columns,
        out_specs=pl.BlockSpec(memory_space=pltpu.HBM),
        scratch_shapes=[pltpu.VMEM((length, features), BF16), pltpu.SemaphoreType.DMA((features // CHUNK,))],
    )
    grad_value, grad_filt = call(
        unpack_grads, [signal, jax.ShapeDtypeStruct((length, width), F32)], got, t["spread"].T
    )
    return (mixed[None], grad_query[None], grad_value[None], grad_filt)


def solution(mesh):
    placed = (
        P("dp", "seq", "tensor"),
        P("dp", "seq", "tensor"),
        P("seq", "tensor"),
        P("tensor", None),
        P("dp", "seq", "tensor"),
    )
    return jax.shard_map(
        functools.partial(per_device, count=mesh.shape["tensor"]),
        mesh=mesh,
        in_specs=placed,
        out_specs=(
            P("dp", "seq", "tensor"),
            P("dp", "seq", "tensor"),
            P("dp", "seq", "tensor"),
            P("seq", "tensor"),
        ),
        check_vma=False,
    )
```

```python
import functools
import math

import jax
import jax.numpy as jnp
import ml_dtypes
import numpy as np
from jax import lax
from jax.experimental import pallas as pl
from jax.experimental.pallas import tpu as pltpu
from jax.sharding import PartitionSpec as P

F32 = jnp.float32
BF16 = jnp.bfloat16
DP = 4
SEQ = 32
ROWS = 4
LANES = 128
CHUNK = 256
HALVES = 256
SLOTS = 8
TURN = 22
LATER = 0
HALF = 128


def narrow(table):
    return table.astype(ml_dtypes.bfloat16)


@functools.cache
def tables():
    coarse = np.arange(HALF) + 0.5
    row = np.arange(SEQ * SLOTS)

    def outer(turn):
        place = (row // SLOTS + turn) % SEQ * ROWS + row % SLOTS % ROWS
        angle = 2 * math.pi / 256 * coarse[:, None] * place[None, :]
        full = np.concatenate([np.cos(angle), -np.sin(angle)])
        first = np.where(row[None, :] % SLOTS < ROWS, full, 0.0)
        return first, full - first

    first, second = outer(LATER)
    turned_first, turned_second = outer(TURN)
    fine = np.arange(LANES)
    angle = 2 * math.pi / LANES * np.outer(fine, fine)
    cos, sin = np.cos(angle), np.sin(angle)
    inner = np.block([[cos, -sin], [sin, cos]])
    angle = 2 * math.pi / 32768 * np.outer(coarse, fine)
    twist = np.stack([np.cos(angle), np.sin(angle)]).astype(np.float32)
    spread, turned_spread = np.zeros((256, 256)), np.zeros((256, 256))
    for channel in range(32):
        for slot in range(SLOTS):
            spread[channel * SLOTS + slot, slot * 32 + channel] = 1.0
            turned_spread[channel * SLOTS + slot, slot * 32 + (channel + TURN - LATER) % 32] = 1.0
    return {
        "turned_first": narrow(turned_first),
        "turned_second": narrow(turned_second),
        "fwd_second": narrow(second),
        "inv_first": narrow(first.T / 16384),
        "inv_second": narrow(second.T / 16384),
        "inner": narrow(inner),
        "inner_t": narrow(inner.T),
        "twist": twist,
        "spread": narrow(spread),
        "turned_spread": narrow(turned_spread),
    }


def dot(left, right):
    return jnp.dot(left, right, preferred_element_type=F32)


def lanes(tiles):
    return jnp.concatenate(tiles, axis=1)


def rows(tiles):
    return jnp.concatenate(tiles, axis=0)


def forward(signals, outer_ref, inner_ref, twist_ref):
    count = signals.shape[1] // LANES
    coarse = dot(outer_ref[...], signals)
    cos, sin = lanes([twist_ref[0]] * count), lanes([twist_ref[1]] * count)
    real, imag = coarse[:HALF], coarse[HALF:]
    real, imag = real * cos + imag * sin, imag * cos - real * sin
    cuts = [slice(k * LANES, (k + 1) * LANES) for k in range(count)]
    return dot(rows([lanes([real[:, cut], imag[:, cut]]) for cut in cuts]).astype(BF16), inner_ref[...])


def inverse_inner(spectra, inner_t_ref, twist_ref):
    count = spectra.shape[0] // HALF
    coarse = dot(spectra.astype(BF16), inner_t_ref[...])
    cos, sin = twist_ref[0], twist_ref[1]
    out = []
    for k in range(count):
        real, imag = coarse[k * HALF:(k + 1) * HALF, :LANES], coarse[k * HALF:(k + 1) * HALF, LANES:]
        out.append(rows([real * cos - imag * sin, imag * cos + real * sin]))
    return lanes(out).astype(BF16)


def pack_inputs(values_ref, filt_ref, spread_ref, out_ref):
    dp = lax.axis_index("dp")
    start = pl.multiple_of(dp * LANES, LANES)
    quarter = filt_ref[pl.ds(start, LANES), :].T
    tiles = [values_ref[q * LANES:(q + 1) * LANES, :].T for q in range(ROWS)]
    tiles += [jnp.where(dp == q, quarter, 0.0).astype(BF16) for q in range(DP)]
    for part in range(4):
        block = jnp.concatenate([tile[part * 32:(part + 1) * 32] for tile in tiles], axis=0)
        out_ref[part * 256:(part + 1) * 256, :] = dot(spread_ref[...], block).astype(BF16)


def convolve(got_ref, first_ref, second_ref, inv_ref, inner_ref, inner_t_ref, twist_ref, conv_ref, vspec_ref, fspec_ref):
    size = SEQ * SLOTS
    parts = [got_ref[b * size:(b + 1) * size, :] for b in range(DP)]
    filt = ((parts[0].astype(F32) + parts[1].astype(F32)) + (parts[2].astype(F32) + parts[3].astype(F32))).astype(BF16)
    fspec = forward(filt, second_ref, inner_ref, twist_ref)
    fspec_ref[...] = fspec
    f_real, f_imag = fspec[:, :LANES], fspec[:, LANES:]
    vspec = forward(lanes(parts), first_ref, inner_ref, twist_ref)
    vspec_ref[...] = vspec
    spectra = []
    for b in range(DP):
        v_real, v_imag = vspec[b * HALF:(b + 1) * HALF, :LANES], vspec[b * HALF:(b + 1) * HALF, LANES:]
        spectra.append(lanes([v_real * f_real - v_imag * f_imag, v_real * f_imag + v_imag * f_real]))
    conv = dot(inv_ref[...], inverse_inner(rows(spectra), inner_t_ref, twist_ref))
    for b in range(DP):
        conv_ref[b * size:(b + 1) * size, :] = conv[:, b * LANES:(b + 1) * LANES].astype(BF16)


def partial_grads(cot_ref, *refs):
    *refs, buffer, sems = refs
    count = len(refs) // 2
    copies = [
        pltpu.make_async_copy(cot_ref.at[pl.ds(k * HALVES, HALVES)], buffer.at[pl.ds(k * HALVES, HALVES)], sems.at[k])
        for k in range(2)
    ]
    for copy in copies:
        copy.start()
    columns = rows([ref[...] for ref in refs[:count]])
    for k, copy in enumerate(copies):
        block = slice(k * HALVES, (k + 1) * HALVES)
        copy.wait()
        out = lax.dot_general(
            buffer[block, :], columns, (((1,), (1,)), ((), ())), preferred_element_type=F32
        ).astype(BF16)
        for group, ref in enumerate(refs[count:]):
            ref[block, :] = out[:, group * LANES:(group + 1) * LANES]


def pack_grads(*refs):
    query_ref, conv_ref, spread_ref = refs[:3]
    pieces, (out_ref, grad_ref) = refs[3:-2], refs[-2:]
    grad = pieces[0][...].astype(F32)
    for piece in pieces[1:]:
        grad = grad + piece[...].astype(F32)
    grad_ref[...] = grad
    grad_conv = grad * query_ref[...].astype(F32)
    tiles = [grad_conv[q * LANES:(q + 1) * LANES, :].T.astype(BF16) for q in range(ROWS)]
    spread = spread_ref[:, 128:]
    for part in range(4):
        block = jnp.concatenate([tile[part * 32:(part + 1) * 32] for tile in tiles], axis=0)
        out_ref[part * 256:(part + 1) * 256, :] = (
            dot(spread, block) + conv_ref[part * 256:(part + 1) * 256, :].astype(F32)
        ).astype(BF16)


def gather_half(got_ref, gather):
    blocks = [dot(gather, got_ref[part * 256:(part + 1) * 256, :]) for part in range(4)]
    return [
        jnp.concatenate([block[q * 32:(q + 1) * 32] for block in blocks], axis=0).T for q in range(gather.shape[0] // 32)
    ]


def unpack_conv(got_ref, query_ref, grad_ref, gather_ref, gated_ref, grad_query_ref):
    for q, conv in enumerate(gather_half(got_ref, gather_ref[:128, :])):
        cut = slice(q * LANES, (q + 1) * LANES)
        gated_ref[cut, :] = (query_ref[cut, :].astype(F32) * conv).astype(BF16)
        grad_query_ref[cut, :] = (grad_ref[cut, :] * conv).astype(BF16)


def correlate(
    got_ref, vspec_ref, fspec_ref, second_ref, inv_first_ref, inv_second_ref, inner_ref, inner_t_ref, twist_ref, out_ref
):
    size = SEQ * SLOTS
    f_real, f_imag = fspec_ref[:, :LANES], fspec_ref[:, LANES:]
    sum_real = sum_imag = None
    spec = forward(
        lanes([got_ref[b * size:(b + 1) * size, :] for b in range(DP)]), second_ref, inner_ref, twist_ref
    )
    spectra = []
    for b in range(DP):
        block = slice(b * HALF, (b + 1) * HALF)
        real, imag = spec[block, :LANES], spec[block, LANES:]
        v_real, v_imag = vspec_ref[block, :LANES], vspec_ref[block, LANES:]
        part_real = real * v_real + imag * v_imag
        part_imag = imag * v_real - real * v_imag
        sum_real = part_real if b == 0 else sum_real + part_real
        sum_imag = part_imag if b == 0 else sum_imag + part_imag
        spectra.append(lanes([real * f_real + imag * f_imag, imag * f_real - real * f_imag]))
    spectra.append(lanes([sum_real, sum_imag]))
    coarse = inverse_inner(rows(spectra), inner_t_ref, twist_ref)
    cut = DP * LANES
    value = dot(inv_first_ref[...], coarse[:, :cut])
    filt = dot(inv_second_ref[...], coarse[:, cut:])
    for b in range(DP):
        out_ref[b * size:(b + 1) * size, :] = (value[:, b * LANES:(b + 1) * LANES] + filt).astype(BF16)


def project(gated_ref, *refs):
    *refs, out_ref, buffer, sems = refs
    count = len(refs)
    length = buffer.shape[0]
    rank = lax.axis_index("tensor")
    starts = [pl.multiple_of((rank + count - d) % count * length, length) for d in range(count)]
    gated = lanes([gated_ref[pl.ds(start, length), :] for start in starts])
    copies = []
    for k in range(buffer.shape[1] // CHUNK):
        cut = slice(k * CHUNK, (k + 1) * CHUNK)
        buffer[:, cut] = dot(gated, rows([ref[:, cut] for ref in refs])).astype(BF16)
        cut = pl.ds(k * CHUNK, CHUNK)
        copies.append(pltpu.make_async_copy(buffer.at[:, cut], out_ref.at[:, cut], sems.at[k]))
        copies[-1].start()
    for copy in copies:
        copy.wait()


def unpack_grads(got_ref, gather_ref, value_ref, filt_ref, value, filt, sems):
    blocks = [dot(gather_ref[...], got_ref[part * 256:(part + 1) * 256, :]) for part in range(4)]
    copies = []
    for slot in list(range(ROWS, SLOTS)) + list(range(ROWS)):
        buffer, ref = (value, value_ref) if slot < ROWS else (filt, filt_ref)
        tile = jnp.concatenate([block[slot * 32:(slot + 1) * 32] for block in blocks], axis=0).T
        start = slot % ROWS * LANES
        buffer[start:start + LANES, :] = tile.astype(buffer.dtype)
        cut = pl.ds(start, LANES)
        copies.append(pltpu.make_async_copy(buffer.at[cut], ref.at[cut], sems.at[slot]))
        copies[-1].start()
    for copy in copies:
        copy.wait()


COVER = pl.CostEstimate(flops=40_000_000_000, transcendentals=0, bytes_accessed=40_000_000)
COVERS = {"pack_inputs": COVER, "partial_grads": COVER}


def call(kernel, outs, *operands, **options):
    return pl.pallas_call(
        kernel,
        out_shape=outs,
        **options,
        name=kernel.__name__,
        cost_estimate=COVERS.get(kernel.__name__),
        compiler_params=pltpu.CompilerParams(vmem_limit_bytes=40 * 1024 * 1024),
    )(*operands)


def exchange(message, turn=LATER):
    shape = message.shape
    message = message.reshape(DP * SEQ, SLOTS, LANES)
    group = [b * SEQ + (s + turn) % SEQ for b in range(DP) for s in range(SEQ)]
    return lax.all_to_all(
        message, ("dp", "seq"), split_axis=0, concat_axis=0, tiled=True, axis_index_groups=[group] if turn else None
    ).reshape(shape)


def shifted(array, distance, count):
    return lax.ppermute(array, "tensor", [(i, (i + distance) % count) for i in range(count)])


def per_device(queries, values, filt, w_out, cotangent, count):
    t = tables()
    query = queries[0]
    length, width = query.shape
    features = cotangent.shape[2]
    rank = lax.axis_index("tensor")
    vmem = pl.BlockSpec(memory_space=pltpu.VMEM)
    message = jax.ShapeDtypeStruct((DP * SEQ * SLOTS, LANES), BF16)
    signal = jax.ShapeDtypeStruct((length, width), BF16)

    columns = []
    for d in range(count):
        piece = lax.dynamic_slice(w_out, (0, (rank + d) % count * features), (width, features))
        columns.append(shifted(piece, d, count) if d else piece)

    got = exchange(call(pack_inputs, message, values[0], filt, t["turned_spread"]), TURN)
    conv, value_spec, filt_spec = call(
        convolve,
        [
            message,
            jax.ShapeDtypeStruct((DP * HALF, 2 * LANES), F32),
            jax.ShapeDtypeStruct((HALF, 2 * LANES), F32),
        ],
        got, t["turned_first"], t["turned_second"], t["inv_first"], t["inner"], t["inner_t"], t["twist"],
    )
    partial = call(
        partial_grads, [signal] * count, pltpu.with_memory_space_constraint(cotangent[0], pltpu.HBM), *columns,
        in_specs=[pl.BlockSpec(memory_space=pltpu.HBM)] + [vmem] * count,
        scratch_shapes=[pltpu.VMEM((length, features), BF16), pltpu.SemaphoreType.DMA((2,))],
    )
    partial = [shifted(p, -d, count) if d else p for d, p in enumerate(partial)]
    outgoing, grad_gated = call(
        pack_grads, [message, jax.ShapeDtypeStruct((length, width), F32)], query, conv, t["spread"], *partial
    )
    got = exchange(outgoing)
    gated, grad_query = call(unpack_conv, [signal, signal], got, query, grad_gated, t["spread"].T)
    gathered = lax.all_gather(gated, "tensor", axis=0, tiled=True)
    got = exchange(
        call(
            correlate, message, got, value_spec, filt_spec, t["fwd_second"], t["inv_first"], t["inv_second"],
            t["inner"], t["inner_t"], t["twist"],
        )
    )
    mixed = call(
        project, jax.ShapeDtypeStruct((length, features), BF16), gathered, *columns,
        out_specs=pl.BlockSpec(memory_space=pltpu.HBM),
        scratch_shapes=[pltpu.VMEM((length, features), BF16), pltpu.SemaphoreType.DMA((features // CHUNK,))],
    )
    grad_value, grad_filt = call(
        unpack_grads, [signal, jax.ShapeDtypeStruct((length, width), F32)], got, t["spread"].T,
        out_specs=[pl.BlockSpec(memory_space=pltpu.HBM)] * 2,
        scratch_shapes=[
            pltpu.VMEM((length, width), BF16), pltpu.VMEM((length, width), F32), pltpu.SemaphoreType.DMA((SLOTS,))
        ],
    )
    return (mixed[None], grad_query[None], grad_value[None], grad_filt)


def solution(mesh):
    placed = (
        P("dp", "seq", "tensor"),
        P("dp", "seq", "tensor"),
        P("seq", "tensor"),
        P("tensor", None),
        P("dp", "seq", "tensor"),
    )
    return jax.shard_map(
        functools.partial(per_device, count=mesh.shape["tensor"]),
        mesh=mesh,
        in_specs=placed,
        out_specs=(
            P("dp", "seq", "tensor"),
            P("dp", "seq", "tensor"),
            P("dp", "seq", "tensor"),
            P("seq", "tensor"),
        ),
        check_vma=False,
    )
```

```python
import functools
import math

import jax
import jax.numpy as jnp
import ml_dtypes
import numpy as np
from jax import lax
from jax.experimental import pallas as pl
from jax.experimental.pallas import tpu as pltpu
from jax.sharding import PartitionSpec as P

F32 = jnp.float32
BF16 = jnp.bfloat16
DP = 4
SEQ = 32
ROWS = 4
LANES = 128
CHUNK = 128
HALVES = 256
SLOTS = 8
TURN = 22
LATER = 0
HALF = 128


def narrow(table):
    return table.astype(ml_dtypes.bfloat16)


@functools.cache
def tables():
    coarse = np.arange(HALF) + 0.5
    row = np.arange(SEQ * SLOTS)

    def outer(turn):
        place = (row // SLOTS + turn) % SEQ * ROWS + row % SLOTS % ROWS
        angle = 2 * math.pi / 256 * coarse[:, None] * place[None, :]
        full = np.concatenate([np.cos(angle), -np.sin(angle)])
        first = np.where(row[None, :] % SLOTS < ROWS, full, 0.0)
        return first, full - first

    first, second = outer(LATER)
    turned_first, turned_second = outer(TURN)
    fine = np.arange(LANES)
    angle = 2 * math.pi / LANES * np.outer(fine, fine)
    cos, sin = np.cos(angle), np.sin(angle)
    inner = np.block([[cos, -sin], [sin, cos]])
    angle = 2 * math.pi / 32768 * np.outer(coarse, fine)
    twist = np.stack([np.cos(angle), np.sin(angle)]).astype(np.float32)
    spread, turned_spread = np.zeros((256, 256)), np.zeros((256, 256))
    for channel in range(32):
        for slot in range(SLOTS):
            spread[channel * SLOTS + slot, slot * 32 + channel] = 1.0
            turned_spread[channel * SLOTS + slot, slot * 32 + (channel + TURN - LATER) % 32] = 1.0
    return {
        "turned_first": narrow(turned_first),
        "turned_second": narrow(turned_second),
        "fwd_second": narrow(second),
        "inv_first": narrow(first.T / 16384),
        "inv_second": narrow(second.T / 16384),
        "inner": narrow(inner),
        "inner_t": narrow(inner.T),
        "twist": twist,
        "spread": narrow(spread),
        "turned_spread": narrow(turned_spread),
    }


def dot(left, right):
    return jnp.dot(left, right, preferred_element_type=F32)


def lanes(tiles):
    return jnp.concatenate(tiles, axis=1)


def rows(tiles):
    return jnp.concatenate(tiles, axis=0)


def forward(signals, outer_ref, inner_ref, twist_ref):
    count = signals.shape[1] // LANES
    coarse = dot(outer_ref[...], signals)
    cos, sin = lanes([twist_ref[0]] * count), lanes([twist_ref[1]] * count)
    real, imag = coarse[:HALF], coarse[HALF:]
    real, imag = real * cos + imag * sin, imag * cos - real * sin
    cuts = [slice(k * LANES, (k + 1) * LANES) for k in range(count)]
    return dot(rows([lanes([real[:, cut], imag[:, cut]]) for cut in cuts]).astype(BF16), inner_ref[...])


def inverse_inner(spectra, inner_t_ref, twist_ref):
    count = spectra.shape[0] // HALF
    coarse = dot(spectra.astype(BF16), inner_t_ref[...])
    cos, sin = twist_ref[0], twist_ref[1]
    out = []
    for k in range(count):
        real, imag = coarse[k * HALF:(k + 1) * HALF, :LANES], coarse[k * HALF:(k + 1) * HALF, LANES:]
        out.append(rows([real * cos - imag * sin, imag * cos + real * sin]))
    return lanes(out).astype(BF16)


def pack_inputs(values_ref, filt_ref, spread_ref, out_ref):
    dp = lax.axis_index("dp")
    start = pl.multiple_of(dp * LANES, LANES)
    quarter = filt_ref[pl.ds(start, LANES), :].T
    tiles = [values_ref[q * LANES:(q + 1) * LANES, :].T for q in range(ROWS)]
    tiles += [jnp.where(dp == q, quarter, 0.0).astype(BF16) for q in range(DP)]
    for part in range(4):
        block = jnp.concatenate([tile[part * 32:(part + 1) * 32] for tile in tiles], axis=0)
        out_ref[part * 256:(part + 1) * 256, :] = dot(spread_ref[...], block).astype(BF16)


def convolve(got_ref, first_ref, second_ref, inv_ref, inner_ref, inner_t_ref, twist_ref, conv_ref, vspec_ref, fspec_ref):
    size = SEQ * SLOTS
    parts = [got_ref[b * size:(b + 1) * size, :] for b in range(DP)]
    filt = ((parts[0].astype(F32) + parts[1].astype(F32)) + (parts[2].astype(F32) + parts[3].astype(F32))).astype(BF16)
    fspec = forward(filt, second_ref, inner_ref, twist_ref)
    fspec_ref[...] = fspec
    f_real, f_imag = fspec[:, :LANES], fspec[:, LANES:]
    vspec = forward(lanes(parts), first_ref, inner_ref, twist_ref)
    vspec_ref[...] = vspec
    spectra = []
    for b in range(DP):
        v_real, v_imag = vspec[b * HALF:(b + 1) * HALF, :LANES], vspec[b * HALF:(b + 1) * HALF, LANES:]
        spectra.append(lanes([v_real * f_real - v_imag * f_imag, v_real * f_imag + v_imag * f_real]))
    conv = dot(inv_ref[...], inverse_inner(rows(spectra), inner_t_ref, twist_ref))
    for b in range(DP):
        conv_ref[b * size:(b + 1) * size, :] = conv[:, b * LANES:(b + 1) * LANES].astype(BF16)


def partial_grads(cot_ref, *refs):
    *refs, buffer, sems = refs
    count = len(refs) // 2
    copies = [
        pltpu.make_async_copy(cot_ref.at[pl.ds(k * HALVES, HALVES)], buffer.at[pl.ds(k * HALVES, HALVES)], sems.at[k])
        for k in range(2)
    ]
    for copy in copies:
        copy.start()
    columns = rows([ref[...] for ref in refs[:count]])
    for k, copy in enumerate(copies):
        block = slice(k * HALVES, (k + 1) * HALVES)
        copy.wait()
        out = lax.dot_general(
            buffer[block, :], columns, (((1,), (1,)), ((), ())), preferred_element_type=F32
        ).astype(BF16)
        for group, ref in enumerate(refs[count:]):
            ref[block, :] = out[:, group * LANES:(group + 1) * LANES]


def pack_grads(*refs):
    query_ref, conv_ref, spread_ref = refs[:3]
    pieces, (out_ref, grad_ref) = refs[3:-2], refs[-2:]
    grad = pieces[0][...].astype(F32)
    for piece in pieces[1:]:
        grad = grad + piece[...].astype(F32)
    grad_ref[...] = grad
    grad_conv = grad * query_ref[...].astype(F32)
    tiles = [grad_conv[q * LANES:(q + 1) * LANES, :].T.astype(BF16) for q in range(ROWS)]
    spread = spread_ref[:, 128:]
    for part in range(4):
        block = jnp.concatenate([tile[part * 32:(part + 1) * 32] for tile in tiles], axis=0)
        out_ref[part * 256:(part + 1) * 256, :] = (
            dot(spread, block) + conv_ref[part * 256:(part + 1) * 256, :].astype(F32)
        ).astype(BF16)


def gather_half(got_ref, gather):
    blocks = [dot(gather, got_ref[part * 256:(part + 1) * 256, :]) for part in range(4)]
    return [
        jnp.concatenate([block[q * 32:(q + 1) * 32] for block in blocks], axis=0).T for q in range(gather.shape[0] // 32)
    ]


def unpack_conv(got_ref, query_ref, grad_ref, gather_ref, gated_ref, grad_query_ref):
    for q, conv in enumerate(gather_half(got_ref, gather_ref[:128, :])):
        cut = slice(q * LANES, (q + 1) * LANES)
        gated_ref[cut, :] = (query_ref[cut, :].astype(F32) * conv).astype(BF16)
        grad_query_ref[cut, :] = (grad_ref[cut, :] * conv).astype(BF16)


def correlate(
    got_ref, vspec_ref, fspec_ref, second_ref, inv_first_ref, inv_second_ref, inner_ref, inner_t_ref, twist_ref, out_ref
):
    size = SEQ * SLOTS
    f_real, f_imag = fspec_ref[:, :LANES], fspec_ref[:, LANES:]
    sum_real = sum_imag = None
    spec = forward(
        lanes([got_ref[b * size:(b + 1) * size, :] for b in range(DP)]), second_ref, inner_ref, twist_ref
    )
    spectra = []
    for b in range(DP):
        block = slice(b * HALF, (b + 1) * HALF)
        real, imag = spec[block, :LANES], spec[block, LANES:]
        v_real, v_imag = vspec_ref[block, :LANES], vspec_ref[block, LANES:]
        part_real = real * v_real + imag * v_imag
        part_imag = imag * v_real - real * v_imag
        sum_real = part_real if b == 0 else sum_real + part_real
        sum_imag = part_imag if b == 0 else sum_imag + part_imag
        spectra.append(lanes([real * f_real + imag * f_imag, imag * f_real - real * f_imag]))
    spectra.append(lanes([sum_real, sum_imag]))
    coarse = inverse_inner(rows(spectra), inner_t_ref, twist_ref)
    cut = DP * LANES
    value = dot(inv_first_ref[...], coarse[:, :cut])
    filt = dot(inv_second_ref[...], coarse[:, cut:])
    for b in range(DP):
        out_ref[b * size:(b + 1) * size, :] = (value[:, b * LANES:(b + 1) * LANES] + filt).astype(BF16)


def project(gated_ref, *refs):
    *refs, out_ref, buffer, sems = refs
    count = len(refs)
    length = buffer.shape[0]
    rank = lax.axis_index("tensor")
    starts = [pl.multiple_of((rank + count - d) % count * length, length) for d in range(count)]
    gated = lanes([gated_ref[pl.ds(start, length), :] for start in starts])
    copies = []
    for k in range(buffer.shape[1] // CHUNK):
        cut = slice(k * CHUNK, (k + 1) * CHUNK)
        buffer[:, cut] = dot(gated, rows([ref[:, cut] for ref in refs])).astype(BF16)
        cut = pl.ds(k * CHUNK, CHUNK)
        copies.append(pltpu.make_async_copy(buffer.at[:, cut], out_ref.at[:, cut], sems.at[k]))
        copies[-1].start()
    for copy in copies:
        copy.wait()


def unpack_grads(got_ref, gather_ref, value_ref, filt_ref, value, filt, sems):
    blocks = [dot(gather_ref[...], got_ref[part * 256:(part + 1) * 256, :]) for part in range(4)]
    copies = []
    for slot in list(range(ROWS, SLOTS)) + list(range(ROWS)):
        buffer, ref = (value, value_ref) if slot < ROWS else (filt, filt_ref)
        tile = jnp.concatenate([block[slot * 32:(slot + 1) * 32] for block in blocks], axis=0).T
        start = slot % ROWS * LANES
        buffer[start:start + LANES, :] = tile.astype(buffer.dtype)
        cut = pl.ds(start, LANES)
        copies.append(pltpu.make_async_copy(buffer.at[cut], ref.at[cut], sems.at[slot]))
        copies[-1].start()
    for copy in copies:
        copy.wait()


COVER = pl.CostEstimate(flops=40_000_000_000, transcendentals=0, bytes_accessed=40_000_000)
COVERS = {"pack_inputs": COVER, "partial_grads": COVER}


def call(kernel, outs, *operands, **options):
    return pl.pallas_call(
        kernel,
        out_shape=outs,
        **options,
        name=kernel.__name__,
        cost_estimate=COVERS.get(kernel.__name__),
        compiler_params=pltpu.CompilerParams(vmem_limit_bytes=40 * 1024 * 1024),
    )(*operands)


def exchange(message, turn=LATER):
    shape = message.shape
    message = message.reshape(DP * SEQ, SLOTS, LANES)
    group = [b * SEQ + (s + turn) % SEQ for b in range(DP) for s in range(SEQ)]
    return lax.all_to_all(
        message, ("dp", "seq"), split_axis=0, concat_axis=0, tiled=True, axis_index_groups=[group] if turn else None
    ).reshape(shape)


def shifted(array, distance, count):
    return lax.ppermute(array, "tensor", [(i, (i + distance) % count) for i in range(count)])


def per_device(queries, values, filt, w_out, cotangent, count):
    t = tables()
    query = queries[0]
    length, width = query.shape
    features = cotangent.shape[2]
    rank = lax.axis_index("tensor")
    vmem = pl.BlockSpec(memory_space=pltpu.VMEM)
    message = jax.ShapeDtypeStruct((DP * SEQ * SLOTS, LANES), BF16)
    signal = jax.ShapeDtypeStruct((length, width), BF16)

    columns = []
    for d in range(count):
        piece = lax.dynamic_slice(w_out, (0, (rank + d) % count * features), (width, features))
        columns.append(shifted(piece, d, count) if d else piece)

    got = exchange(call(pack_inputs, message, values[0], filt, t["turned_spread"]), TURN)
    conv, value_spec, filt_spec = call(
        convolve,
        [
            message,
            jax.ShapeDtypeStruct((DP * HALF, 2 * LANES), F32),
            jax.ShapeDtypeStruct((HALF, 2 * LANES), F32),
        ],
        got, t["turned_first"], t["turned_second"], t["inv_first"], t["inner"], t["inner_t"], t["twist"],
    )
    partial = call(
        partial_grads, [signal] * count, pltpu.with_memory_space_constraint(cotangent[0], pltpu.HBM), *columns,
        in_specs=[pl.BlockSpec(memory_space=pltpu.HBM)] + [vmem] * count,
        scratch_shapes=[pltpu.VMEM((length, features), BF16), pltpu.SemaphoreType.DMA((2,))],
    )
    partial = [shifted(p, -d, count) if d else p for d, p in enumerate(partial)]
    outgoing, grad_gated = call(
        pack_grads, [message, jax.ShapeDtypeStruct((length, width), F32)], query, conv, t["spread"], *partial
    )
    got = exchange(outgoing)
    gated, grad_query = call(unpack_conv, [signal, signal], got, query, grad_gated, t["spread"].T)
    gathered = lax.all_gather(gated, "tensor", axis=0, tiled=True)
    got = exchange(
        call(
            correlate, message, got, value_spec, filt_spec, t["fwd_second"], t["inv_first"], t["inv_second"],
            t["inner"], t["inner_t"], t["twist"],
        )
    )
    mixed = call(
        project, jax.ShapeDtypeStruct((length, features), BF16), gathered, *columns,
        out_specs=pl.BlockSpec(memory_space=pltpu.HBM),
        scratch_shapes=[pltpu.VMEM((length, features), BF16), pltpu.SemaphoreType.DMA((features // CHUNK,))],
    )
    grad_value, grad_filt = call(
        unpack_grads, [signal, jax.ShapeDtypeStruct((length, width), F32)], got, t["spread"].T,
        out_specs=[pl.BlockSpec(memory_space=pltpu.HBM)] * 2,
        scratch_shapes=[
            pltpu.VMEM((length, width), BF16), pltpu.VMEM((length, width), F32), pltpu.SemaphoreType.DMA((SLOTS,))
        ],
    )
    return (mixed[None], grad_query[None], grad_value[None], grad_filt)


def solution(mesh):
    placed = (
        P("dp", "seq", "tensor"),
        P("dp", "seq", "tensor"),
        P("seq", "tensor"),
        P("tensor", None),
        P("dp", "seq", "tensor"),
    )
    return jax.shard_map(
        functools.partial(per_device, count=mesh.shape["tensor"]),
        mesh=mesh,
        in_specs=placed,
        out_specs=(
            P("dp", "seq", "tensor"),
            P("dp", "seq", "tensor"),
            P("dp", "seq", "tensor"),
            P("seq", "tensor"),
        ),
        check_vma=False,
    )
```
